32 devices in a mesh: dp: 8 (over y, x, core), seq: 4 (over z).
Axes of the slice: x: 2, y: 2, z: 4, core: 2. Of those that a mesh axis runs over, the one named last changes fastest.
Arguments:
- tokens: bfloat16 [8, 2, 1024, 768], P('dp', None, 'seq'), may hold values from -6 to 6
- cotangent: bfloat16 [8, 2, 1024, 768], P('dp', None, 'seq'), may hold values from -6 to 6
- lengths: int32 [8, 2, 5], P('dp'), may hold values from 0 to 577, as said below
- gain_one: bfloat16 [768], P(('dp', 'seq')), may hold values from 0.25 to 1.75
- shift_one: bfloat16 [768], P(('dp', 'seq')), may hold values from -4 to 4
- qkv_weight: bfloat16 [768, 2304], P(('dp', 'seq')), may hold values from -0.21875 to 0.21875
- query_bias: bfloat16 [768], P(('dp', 'seq')), may hold values from -4 to 4
- value_bias: bfloat16 [768], P(('dp', 'seq')), may hold values from -0.75 to 0.75
- proj_weight: bfloat16 [768, 768], P(('dp', 'seq')), may hold values from -1.75 to 1.75
- proj_bias: bfloat16 [768], P(('dp', 'seq')), may hold values from -3 to 3
- gain_two: bfloat16 [768], P(('dp', 'seq')), may hold values from 0.25 to 1.75
- shift_two: bfloat16 [768], P(('dp', 'seq')), may hold values from -4 to 4
- up_weight: bfloat16 [768, 3072], P(('dp', 'seq')), may hold values from -0.21875 to 0.21875
- up_bias: bfloat16 [3072], P(('dp', 'seq')), may hold values from -6 to 6
- down_weight: bfloat16 [3072, 768], P(('dp', 'seq')), may hold values from -0.109375 to 0.109375
- down_bias: bfloat16 [768], P(('dp', 'seq')), may hold values from -3 to 3
Outputs:
- block_out: bfloat16 [8, 2, 1024, 768], P('dp', None, 'seq')
- input_grad: bfloat16 [8, 2, 1024, 768], P('dp', None, 'seq')
- gain_one_grad: float32 [768], P(('dp', 'seq'))
- shift_one_grad: float32 [768], P(('dp', 'seq'))
- qkv_weight_grad: float32 [768, 2304], P(('dp', 'seq'))
- query_bias_grad: float32 [768], P(('dp', 'seq'))
- value_bias_grad: float32 [768], P(('dp', 'seq'))
- proj_weight_grad: float32 [768, 768], P(('dp', 'seq'))
- proj_bias_grad: float32 [768], P(('dp', 'seq'))
- gain_two_grad: float32 [768], P(('dp', 'seq'))
- shift_two_grad: float32 [768], P(('dp', 'seq'))
- up_weight_grad: float32 [768, 3072], P(('dp', 'seq'))
- up_bias_grad: float32 [3072], P(('dp', 'seq'))
- down_weight_grad: float32 [3072, 768], P(('dp', 'seq'))
- down_bias_grad: float32 [768], P(('dp', 'seq'))
The draws below stay inside these ranges and needn't reach their ends.
Inputs may be any that keep to these rules, and one draw needn't show every extreme that they name: `lengths`: each of the 2 packs of an index of dp holds either 5 images of length 197, or 1 image of length 577 followed by slots of length 0; the kind of each pack is random, except that pack 0 of index 0 is of the first kind and pack 1 of index 0 of the second.
All inputs are finite; a program needn't handle non-finite values.
Results may differ from the reference program's by a relative error of at most 0.012.
Values may be sent and summed in bfloat16 or wider, within the bound.
No kernel may reach another device: no remote copies, remote signals or barrier semaphores. Data moves between devices by JAX's collectives and lax.ppermute only.
A program may use at most 192 MiB of HBM per device.

```python
import math
import jax
import jax.numpy as jnp
from jax import lax

D = 768
H = 12
HD = 64
FF = 3072
MB = 2
PACK = 1024
SHORT_VALID = 197
LONG_VALID = 577
SLOTS = 5
LONG_COUNT = 1
QBLOCK = 512
N_DP = 8


def draw_lengths(key, part):
    kinds = jax.random.randint(key, (N_DP * MB,), 0, 2).astype(jnp.int32)
    kinds = kinds.at[0].set(0).at[1].set(1)
    places = jnp.arange(SLOTS, dtype=jnp.int32)
    short_row = jnp.full((SLOTS,), SHORT_VALID, jnp.int32)
    long_row = jnp.where(places < LONG_COUNT, LONG_VALID, 0).astype(jnp.int32)
    chosen = jnp.where(kinds[:, None] == 1, long_row[None, :], short_row[None, :])
    return chosen.reshape(N_DP, MB, SLOTS).astype(jnp.int32)


def strengthened(values, rng, source, target, shards_of, factor):
    def block_of(position):
        return (jnp.arange(values.shape[position]) // (values.shape[position] // shards_of)).reshape((-1,) + (1,) * (values.ndim - 1 - position))

    first = jax.random.permutation(rng, shards_of)[block_of(target)]
    other_side = (block_of(target) + shards_of // 2) % shards_of
    return jnp.where((block_of(source) == first) | (block_of(source) == other_side), factor * values, values)


def block_scale(own_key, extent, shards, least, high):
    level, own = 1.0, jax.random.fold_in(own_key, 6)
    for position, blocks in shards:
        heights = jnp.exp(jax.random.uniform(jax.random.fold_in(own, position), (blocks,), jnp.float32, least / len(shards), high / len(shards)))
        level = level * jnp.repeat(heights, extent[position] // blocks).reshape([-1 if axis == position else 1 for axis in range(len(extent))])
    return level


def gaussian(stream_key, extent, width, reach, split=(), kind=jnp.bfloat16):
    level = block_scale(stream_key, extent, split, -0.22, 0.18) if split else 1.0
    drawn = jax.random.normal(stream_key, extent, jnp.float32) * width * level
    return jnp.minimum(jnp.maximum(drawn, -reach), reach).astype(kind)


def heavy_noise(rng, extent, scale, bound, split, heavy, kind=jnp.bfloat16):
    array = scale * jax.random.normal(rng, extent, jnp.float32)
    if split:
        array = array * block_scale(rng, extent, split, -0.22, 0.18)
    return jnp.clip(strengthened(array, jax.random.fold_in(rng, 3), *heavy), -bound, bound).astype(kind)


def setup_inputs(seed: int = 0) -> dict:
    arg_keys = jax.random.split(jax.random.key(seed), 17)
    return {
        "tokens": heavy_noise(arg_keys[0], (N_DP, MB, PACK, D), 1.0, 6.0, ((0, 8), (2, 4)), (0, 3, 8, 2.0)),
        "cotangent": gaussian(arg_keys[1], (N_DP, MB, PACK, D), 1.0, 6.0, ((0, 8), (2, 4))),
        "lengths": draw_lengths(jax.random.fold_in(arg_keys[16], 71), 0),
        "gain_one": jnp.clip(1.0 + 0.15 * jax.random.normal(arg_keys[3], (D,), jnp.float32), 0.25, 1.75).astype(jnp.bfloat16),
        "shift_one": gaussian(arg_keys[4], (D,), 0.3, 4.0, ((0, 32),)),
        "qkv_weight": gaussian(arg_keys[5], (D, 3 * D), D ** -0.5, 0.21875, ((0, 32),)),
        "query_bias": gaussian(arg_keys[6], (D,), 0.3, 4.0, ((0, 32),)),
        "value_bias": gaussian(arg_keys[7], (D,), 0.05, 0.75, ((0, 32),)),
        "proj_weight": gaussian(arg_keys[8], (D, D), (D // 64) ** -0.5, 1.75, ((0, 32),)),
        "proj_bias": gaussian(arg_keys[9], (D,), 0.2, 3.0, ((0, 32),)),
        "gain_two": jnp.clip(1.0 + 0.15 * jax.random.normal(arg_keys[10], (D,), jnp.float32), 0.25, 1.75).astype(jnp.bfloat16),
        "shift_two": gaussian(arg_keys[11], (D,), 0.3, 4.0, ((0, 32),)),
        "up_weight": gaussian(arg_keys[12], (D, FF), D ** -0.5, 0.21875, ((0, 32),)),
        "up_bias": gaussian(arg_keys[13], (FF,), 0.5, 6.0, ((0, 32),)),
        "down_weight": gaussian(arg_keys[14], (FF, D), FF ** -0.5, 0.109375, ((0, 32),)),
        "down_bias": gaussian(arg_keys[15], (D,), 0.2, 3.0, ((0, 32),)),
    }


@jax.custom_vjp
def low(v):
    return lax.optimization_barrier(v.astype(jnp.bfloat16)).astype(jnp.float32)

@jax.custom_vjp
def low_back(v):
    return v

def low_keep(v):
    return (low(v), None)

def low_pass(kept, grad):
    return (grad,)

def back_keep(v):
    return (v, None)

def back_low(kept, grad):
    return (low(grad),)
low.defvjp(low_keep, low_pass)
low_back.defvjp(back_keep, back_low)
tail_cells = 3
masked_score = -1000000000.0
norm_eps = 1e-06
highest = lax.Precision.HIGHEST

def layer_norm(values, gain, shift):
    center = values - lax.optimization_barrier(jnp.mean(values, axis=-1, keepdims=True))
    spread = lax.optimization_barrier(jnp.mean(center * center, axis=-1, keepdims=True))
    return center * lax.rsqrt(spread + norm_eps) * gain + shift

def slot_numbers(lens, total):
    widths = jnp.where(lens > 0, lens + tail_cells, 0).astype(jnp.int32)
    starts = (jnp.cumsum(widths) - widths).astype(jnp.int32)
    places = jnp.arange(total, dtype=jnp.int32)
    inside = (places[None, :] >= starts[:, None]) & (places[None, :] < (starts + lens)[:, None])
    labels = jnp.arange(lens.shape[0], dtype=jnp.int32) + 1
    return (lax.optimization_barrier(jnp.sum(jnp.where(inside, labels[:, None], 0), axis=0)) - 1).astype(jnp.int32)

def attention(queries, keys, values, slots):
    scale = 1.0 / math.sqrt(HD)
    key_heads = keys.reshape(PACK, H, HD)
    value_heads = values.reshape(PACK, H, HD)
    query_blocks = queries.reshape(PACK // QBLOCK, QBLOCK, H, HD)
    slot_blocks = slots.reshape(PACK // QBLOCK, QBLOCK)

    def one_block(pair):
        query_block, slot_block = pair
        scores = jnp.einsum('qhd,khd->hqk', query_block, key_heads, precision=highest) * scale
        scores = jnp.where((slot_block[:, None] == slots[None, :])[None], scores, masked_score)
        scores = low_back(scores)
        weights = low(jax.nn.softmax(scores, axis=-1))
        return jnp.einsum('hqk,khd->qhd', weights, value_heads, precision=highest)
    mixed = lax.map(jax.checkpoint(one_block), (query_blocks, slot_blocks))
    return mixed.reshape(PACK, D)

def block(inputs, slots, params):
    gain_one, shift_one, qkv_weight, query_bias, value_bias, proj_weight, proj_bias, gain_two, shift_two, up_weight, up_bias, down_weight, down_bias = params
    first_in = low(layer_norm(inputs, gain_one, shift_one))
    mixed_qkv = jnp.dot(first_in, qkv_weight, precision=highest)
    queries = low_back(low(mixed_qkv[:, 0:D] + query_bias))
    keys = low_back(low(mixed_qkv[:, D:2 * D]))
    values = low_back(low(mixed_qkv[:, 2 * D:3 * D] + value_bias))
    attended = low_back(low(attention(queries, keys, values, slots)))
    middle = inputs + low_back(jnp.dot(attended, proj_weight, precision=highest) + proj_bias)
    second_in = low(layer_norm(middle, gain_two, shift_two))
    hidden = low_back(jnp.dot(second_in, up_weight, precision=highest) + up_bias)
    active = low(jax.nn.gelu(hidden, approximate=False))
    return middle + low_back(jnp.dot(active, down_weight, precision=highest) + down_bias)

def reference(tokens, cotangent, lengths, gain_one, shift_one, qkv_weight, query_bias, value_bias, proj_weight, proj_bias, gain_two, shift_two, up_weight, up_bias, down_weight, down_bias):
    params = tuple((item.astype(jnp.float32) for item in (gain_one, shift_one, qkv_weight, query_bias, value_bias, proj_weight, proj_bias, gain_two, shift_two, up_weight, up_bias, down_weight, down_bias)))
    count = N_DP * MB
    packs = tokens.reshape(count, PACK, D)
    pulls = cotangent.reshape(count, PACK, D)
    lens_all = lengths.reshape(count, SLOTS).astype(jnp.int32)
    zeros = tuple((jnp.zeros(item.shape, jnp.float32) for item in params))

    def one_pack(carry, item):
        pack, pull_in, lens_row = item
        slots = slot_numbers(lens_row, PACK)

        def forward(inputs, *weights):
            return block(inputs, slots, weights)
        output, pull_fn = jax.vjp(forward, pack.astype(jnp.float32), *params)
        pulled = pull_fn(pull_in.astype(jnp.float32))
        carry = tuple((left + right for left, right in zip(carry, pulled[1:])))
        return (carry, (output.astype(jnp.bfloat16), pulled[0].astype(jnp.bfloat16)))
    sums, (outputs, input_grads) = lax.scan(one_pack, zeros, (packs, pulls, lens_all))
    return (outputs.reshape(N_DP, MB, PACK, D), input_grads.reshape(N_DP, MB, PACK, D), sums[0], sums[1], sums[2], sums[3], sums[4], sums[5], sums[6], sums[7], sums[8], sums[9], sums[10], sums[11], sums[12])
```

```python
import math

import jax
import jax.numpy as jnp
from jax import lax
from jax.sharding import PartitionSpec as P

HD = 64
LANES = 128
f32 = jnp.float32
bf16 = jnp.bfloat16

tail_cells = 3
masked_score = -1000000000.0
norm_eps = 1e-06


def dot(left, right, contract):
    return lax.dot_general(left, right, (contract, ((), ())), preferred_element_type=f32)


def layer_norm(values, gain, shift):
    center = values - jnp.mean(values, axis=-1, keepdims=True)
    spread = jnp.mean(center * center, axis=-1, keepdims=True)
    return center * lax.rsqrt(spread + norm_eps) * gain + shift


def gelu_exact(values):
    return jax.nn.gelu(values, approximate=False)


def slot_numbers(lens, places):
    widths = jnp.where(lens > 0, lens + tail_cells, 0)
    starts = jnp.cumsum(widths) - widths
    inside = (places[None, :] >= starts[:, None]) & (places[None, :] < (starts + lens)[:, None])
    labels = jnp.arange(lens.shape[0], dtype=jnp.int32) + 1
    return jnp.sum(jnp.where(inside, labels[:, None], 0), axis=0) - 1


class Grid:
    def __init__(self, dp, seq, micro):
        assert dp & (dp - 1) == 0 and seq == 2 * micro
        self.dp, self.seq, self.micro = dp, seq, micro
        self.bits = [1 << k for k in range(1, dp.bit_length() - 1)]
        self.d = lax.axis_index("dp")
        self.s = lax.axis_index("seq")

    def swap(self, value, bit):
        return lax.ppermute(value, "dp", [(k, k ^ bit) for k in range(self.dp)])

    def turn(self, value, step):
        return lax.ppermute(value, "seq", [(k, (k + step) % self.seq) for k in range(self.seq)])

    def routes(self):
        found = []
        half = self.seq // 2
        for p in range(self.micro):
            pairs = []
            for c in range(self.dp // 2):
                for a in range(2):
                    for s in range(self.seq):
                        m = (s + p) % self.micro
                        k, z = s // half, a * self.micro + m
                        pairs.append(((2 * c + a) * self.seq + s, (2 * c + k) * self.seq + z))
            found.append(pairs)
        return found

    def pick(self, blocks, index):
        return lax.dynamic_index_in_dim(blocks, index, 0, keepdims=False)

    def to_packs(self, blocks):
        got = [
            lax.ppermute(self.pick(blocks, (self.s + p) % self.micro), ("dp", "seq"), pairs)
            for p, pairs in enumerate(self.routes())
        ]
        return jnp.concatenate(got, axis=0)

    def from_packs(self, rows):
        parts = rows.reshape(self.micro, -1, rows.shape[-1])
        got = jnp.stack(
            [
                lax.ppermute(parts[p], ("dp", "seq"), [(b, a) for a, b in pairs])
                for p, pairs in enumerate(self.routes())
            ]
        )
        return jnp.roll(got, self.s % self.micro, axis=0)

    def quarters(self, core):
        own = self.s % self.micro
        half = self.seq // 2
        return [half * core + (own - p) % self.micro for p in range(self.micro)]

    def gather(self, shard, order):
        r, width = shard.shape
        blocks = [shard] + [self.turn(shard, step) for step in range(1, self.seq)]
        stacked = jnp.stack(blocks[::-1] + blocks[::-1])
        value = lax.dynamic_slice_in_dim(
            stacked, (self.seq - 1 - self.s) % self.seq, self.seq, 0
        )
        value = value.reshape(1, self.seq * r * 1, width)
        done = []
        for bit in list(order) + [1]:
            other = self.swap(value, bit)
            low = (self.d & bit) == 0
            at = sum(1 for have in done if have > bit)
            outer = 1 << at
            mine = value.reshape(outer, 1, -1, self.seq * r, width)
            other = other.reshape(outer, 1, -1, self.seq * r, width)
            value = jnp.concatenate(
                [jnp.where(low, mine, other), jnp.where(low, other, mine)], axis=1
            )
            value = value.reshape(-1, self.seq * r, width)
            done.append(bit)
        return value.reshape(-1, width)

    def scatter(self, grad, order):
        width = grad.shape[-1]
        r = grad.shape[0] // (self.dp * self.seq)
        value = grad
        left = sorted([1] + list(order), reverse=True)
        for bit in [1] + list(order):
            at = left.index(bit)
            split = value.reshape(1 << at, 2, -1, width)
            mine = ((self.d & bit) != 0).astype(jnp.int32)
            sent = lax.dynamic_index_in_dim(split, 1 - mine, 1, keepdims=False).astype(bf16)
            kept = lax.dynamic_index_in_dim(split, mine, 1, keepdims=False)
            value = kept.astype(f32) + self.swap(sent, bit).astype(f32)
            left.remove(bit)
        parts = value.reshape(self.seq, r, width)
        total = self.pick(parts, self.s)
        for step in range(1, self.seq):
            sent = self.pick(parts, (self.s + step) % self.seq).astype(bf16)
            total = total + self.turn(sent, step).astype(f32)
        return total


def split_heads(array):
    return array.reshape(array.shape[0], array.shape[1] // HD, HD)


def attend(queries, keys, values, own_slots, slots):
    scale = 1.0 / math.sqrt(HD)
    scores = (
        jnp.einsum("qhd,khd->hqk", split_heads(queries), split_heads(keys), preferred_element_type=f32)
        * scale
    )
    scores = jnp.where((own_slots[:, None] == slots[None, :])[None], scores, masked_score)
    highest = jnp.max(scores, axis=-1, keepdims=True)
    expos = jnp.exp(scores - highest)
    totals = jnp.sum(expos, axis=-1, keepdims=True)
    weights = (expos / totals).astype(bf16)
    mixed = jnp.einsum("hqk,khd->qhd", weights, split_heads(values), preferred_element_type=f32)
    return mixed.astype(bf16).reshape(queries.shape), (highest + jnp.log(totals))


def attend_back(queries, keys, values, grads, logsum, own_slots, slots):
    scale = 1.0 / math.sqrt(HD)
    query_heads, key_heads, value_heads, grad_heads = map(split_heads, (queries, keys, values, grads))
    scores = jnp.einsum("qhd,khd->hqk", query_heads, key_heads, preferred_element_type=f32) * scale
    scores = jnp.where((own_slots[:, None] == slots[None, :])[None], scores, masked_score)
    chances = jnp.exp(scores - logsum)
    grad_chances = jnp.einsum("qhd,khd->hqk", grad_heads, value_heads, preferred_element_type=f32)
    inner = jnp.sum(chances * grad_chances, axis=-1, keepdims=True)
    grad_scores = (chances * (grad_chances - inner)).astype(bf16)
    dq = jnp.einsum("hqk,khd->qhd", grad_scores, key_heads, preferred_element_type=f32) * scale
    dk = jnp.einsum("hqk,qhd->khd", grad_scores, query_heads, preferred_element_type=f32) * scale
    dv = jnp.einsum("hqk,qhd->khd", chances.astype(bf16), grad_heads, preferred_element_type=f32)
    return dq.reshape(queries.shape), dk.reshape(keys.shape), dv.reshape(values.shape)


def local(
    tokens,
    cotangent,
    lengths,
    gain_one,
    shift_one,
    qkv_weight,
    query_bias,
    value_bias,
    proj_weight,
    proj_bias,
    gain_two,
    shift_two,
    up_weight,
    up_bias,
    down_weight,
    down_bias,
    *,
    dp,
    seq,
):
    micro, block, width = tokens.shape[1:]
    grid = Grid(dp, seq, micro)
    r = qkv_weight.shape[0]
    order_a, order_b = grid.bits, grid.bits[::-1]

    small = [gain_one, shift_one, query_bias, value_bias, proj_bias, gain_two, shift_two, down_bias]
    columns = jnp.concatenate([item.reshape(r, 1) for item in small] + [up_bias.reshape(r, -1)], 1)
    columns = jnp.pad(columns, ((0, 0), (0, LANES - columns.shape[1])))
    packed = jnp.concatenate([qkv_weight, columns], axis=1)
    cut = packed.shape[1] // 2 // LANES * LANES

    inputs = grid.to_packs(tokens[0])
    first_half = grid.gather(packed[:, :cut], order_a)
    second_half = grid.gather(packed[:, cut:], order_b)
    grad_out = grid.to_packs(cotangent[0])
    proj_w = grid.gather(proj_weight, order_a)
    up_w = grid.gather(up_weight, order_a)
    down_w = grid.gather(down_weight, order_b)

    columns = second_half[:, 3 * width - cut :].astype(f32)
    rows = columns[:, : len(small)].T
    gain_one_f, shift_one_f, query_b, value_b, proj_b, gain_two_f, shift_two_f, down_b = rows
    up_b = columns[:, len(small) : len(small) + up_bias.shape[0] // r].reshape(-1)
    qkv_w = jnp.concatenate([first_half, second_half[:, : 3 * width - cut]], axis=1)

    core = grid.d % 2
    away = grid.swap(lengths[0], 1)
    lens = jnp.where(grid.s // micro == core, lengths[0], away)
    lens = grid.pick(lens, grid.s % micro)
    spots = jnp.arange(block, dtype=jnp.int32)
    own_slots = slot_numbers(lens, jnp.concatenate([q * block + spots for q in grid.quarters(core)]))
    far_slots = slot_numbers(
        lens, jnp.concatenate([q * block + spots for q in grid.quarters(1 - core)])
    )
    slots = jnp.concatenate([own_slots, far_slots])

    inputs_f = inputs.astype(f32)
    normed, norm_back = jax.vjp(layer_norm, inputs_f, gain_one_f, shift_one_f)
    first_in = normed.astype(bf16)
    qkv = dot(first_in, qkv_w, ((1,), (0,)))
    queries = (qkv[:, :width] + query_b).astype(bf16)
    keys_values = jnp.concatenate(
        [qkv[:, width : 2 * width], qkv[:, 2 * width :] + value_b], axis=1
    ).astype(bf16)
    all_kv = jnp.concatenate([keys_values, grid.swap(keys_values, 1)], axis=0)
    keys, values = all_kv[:, :width], all_kv[:, width:]
    attended, logsum = attend(queries, keys, values, own_slots, slots)

    middle = inputs_f + dot(attended, proj_w, ((1,), (0,))) + proj_b
    second, second_back = jax.vjp(layer_norm, middle, gain_two_f, shift_two_f)
    second_in = second.astype(bf16)
    hidden = dot(second_in, up_w, ((1,), (0,))) + up_b
    active, gelu_back = jax.vjp(gelu_exact, hidden)
    active_in = active.astype(bf16)
    output = (middle + dot(active_in, down_w, ((1,), (0,))) + down_b).astype(bf16)
    block_out = grid.from_packs(output)

    grad_float = grad_out.astype(f32)
    down_weight_grad = grid.scatter(dot(active_in, grad_out, ((0,), (0,))), order_b)
    down_bias_grad = jnp.sum(grad_float, axis=0)
    (grad_hidden,) = gelu_back(dot(grad_out, down_w, ((1,), (1,))))
    grad_hidden_in = grad_hidden.astype(bf16)
    up_weight_grad = grid.scatter(dot(second_in, grad_hidden_in, ((0,), (0,))), order_a)
    up_bias_grad = jnp.sum(grad_hidden_in.astype(f32), axis=0)
    grad_second = dot(grad_hidden_in, up_w, ((1,), (1,)))
    grad_middle_part, gain_two_grad, shift_two_grad = second_back(grad_second)
    grad_middle = grad_float + grad_middle_part
    grad_proj = grad_middle.astype(bf16)
    proj_weight_grad = grid.scatter(dot(attended, grad_proj, ((0,), (0,))), order_a)
    proj_bias_grad = jnp.sum(grad_proj.astype(f32), axis=0)
    grad_attended = dot(grad_proj, proj_w, ((1,), (1,))).astype(bf16)

    dq, dk, dv = attend_back(queries, keys, values, grad_attended, logsum, own_slots, slots)
    dkv = jnp.concatenate([dk, dv], axis=1)
    rows_own = queries.shape[0]
    back = grid.swap(dkv[rows_own:].astype(bf16), 1)
    dqkv = jnp.concatenate([dq, dkv[:rows_own] + back.astype(f32)], axis=1).astype(bf16)
    query_bias_grad = jnp.sum(dqkv[:, :width].astype(f32), axis=0)
    value_bias_grad = jnp.sum(dqkv[:, 2 * width :].astype(f32), axis=0)
    grad_first = dot(dqkv, qkv_w, ((1,), (1,)))
    grad_input_part, gain_one_grad, shift_one_grad = norm_back(grad_first)
    input_grad = grid.from_packs((grad_middle + grad_input_part).astype(bf16))

    qkv_grad = dot(first_in, dqkv, ((0,), (0,)))
    small_grads = [
        gain_one_grad,
        shift_one_grad,
        query_bias_grad,
        value_bias_grad,
        proj_bias_grad,
        gain_two_grad,
        shift_two_grad,
        down_bias_grad,
    ]
    columns = jnp.concatenate(
        [jnp.stack(small_grads, axis=1), up_bias_grad.reshape(width, -1)], axis=1
    )
    taken = columns.shape[1]
    columns = jnp.pad(columns, ((0, 0), (0, LANES - taken)))
    packed = jnp.concatenate(
        [
            grid.scatter(qkv_grad[:, :cut], order_a),
            grid.scatter(jnp.concatenate([qkv_grad[:, cut:], columns], axis=1), order_b),
        ],
        axis=1,
    )
    columns = packed[:, 3 * width :]
    (
        gain_one_grad,
        shift_one_grad,
        query_bias_grad,
        value_bias_grad,
        proj_bias_grad,
        gain_two_grad,
        shift_two_grad,
        down_bias_grad,
    ) = [columns[:, j] for j in range(len(small))]
    up_bias_grad = columns[:, len(small) : taken].reshape(-1)
    return (
        block_out[None],
        input_grad[None],
        gain_one_grad,
        shift_one_grad,
        packed[:, : 3 * width],
        query_bias_grad,
        value_bias_grad,
        proj_weight_grad,
        proj_bias_grad,
        gain_two_grad,
        shift_two_grad,
        up_weight_grad,
        up_bias_grad,
        down_weight_grad,
        down_bias_grad,
    )


def solution(mesh):
    tokens = P("dp", None, "seq", None)
    vector = P(("dp", "seq"))
    matrix = P(("dp", "seq"), None)
    dp, seq = mesh.shape["dp"], mesh.shape["seq"]
    kinds = (
        vector,
        vector,
        matrix,
        vector,
        vector,
        matrix,
        vector,
        vector,
        vector,
        matrix,
        vector,
        matrix,
        vector,
    )
    return jax.shard_map(
        lambda *args: local(*args, dp=dp, seq=seq),
        mesh=mesh,
        in_specs=(tokens, tokens, P("dp", None, None)) + kinds,
        out_specs=(tokens, tokens) + kinds,
        check_vma=False,
    )
```

```python
import math

import jax
import jax.numpy as jnp
from jax import lax
from jax.experimental import pallas as pl
from jax.experimental.pallas import tpu as pltpu
from jax.sharding import PartitionSpec as P

HD = 64
LANES = 128
f32 = jnp.float32
bf16 = jnp.bfloat16

tail_cells = 3
closed = -1e30
norm_eps = 1e-06


def dot(left, right, contract):
    return lax.dot_general(left, right, (contract, ((), ())), preferred_element_type=f32)


def tie(value, *others):
    return lax.optimization_barrier((value,) + others)[0]


def layer_norm(values, gain, shift):
    center = values - jnp.mean(values, axis=-1, keepdims=True)
    spread = jnp.mean(center * center, axis=-1, keepdims=True)
    return center * lax.rsqrt(spread + norm_eps) * gain + shift


def slot_numbers(lens, places):
    widths = jnp.where(lens > 0, lens + tail_cells, 0)
    starts = jnp.cumsum(widths) - widths
    inside = (places[None, :] >= starts[:, None]) & (places[None, :] < (starts + lens)[:, None])
    labels = jnp.arange(lens.shape[0], dtype=jnp.int32) + 1
    return jnp.sum(jnp.where(inside, labels[:, None], 0), axis=0) - 1


class Grid:
    def __init__(self, dp, seq, micro):
        assert dp & (dp - 1) == 0 and seq == 2 * micro
        self.dp, self.seq, self.micro = dp, seq, micro
        self.bits = [1 << k for k in range(1, dp.bit_length() - 1)]
        self.d = lax.axis_index("dp")
        self.s = lax.axis_index("seq")

    def swap(self, value, bit):
        return lax.ppermute(value, "dp", [(k, k ^ bit) for k in range(self.dp)])

    def turn(self, value, step):
        return lax.ppermute(value, "seq", [(k, (k + step) % self.seq) for k in range(self.seq)])

    def routes(self):
        found = []
        half = self.seq // 2
        for p in range(self.micro):
            pairs = []
            for c in range(self.dp // 2):
                for a in range(2):
                    for s in range(self.seq):
                        m = (s + p) % self.micro
                        k, z = s // half, a * self.micro + m
                        pairs.append(((2 * c + a) * self.seq + s, (2 * c + k) * self.seq + z))
            found.append(pairs)
        return found

    def pick(self, blocks, index):
        return lax.dynamic_index_in_dim(blocks, index, 0, keepdims=False)

    def to_packs(self, blocks):
        got = [
            lax.ppermute(self.pick(blocks, (self.s + p) % self.micro), ("dp", "seq"), pairs)
            for p, pairs in enumerate(self.routes())
        ]
        return jnp.concatenate(got, axis=0)

    def from_packs(self, rows):
        parts = rows.reshape(self.micro, -1, rows.shape[-1])
        got = jnp.stack(
            [
                lax.ppermute(parts[p], ("dp", "seq"), [(b, a) for a, b in pairs])
                for p, pairs in enumerate(self.routes())
            ]
        )
        return jnp.roll(got, self.s % self.micro, axis=0)

    def quarters(self, core):
        own = self.s % self.micro
        half = self.seq // 2
        return [half * core + (own - p) % self.micro for p in range(self.micro)]


class Gather:
    def __init__(self, grid, shard, order):
        self.grid, self.shard, self.order, self.done = grid, shard, list(order) + [1], []
        self.rows = grid.seq * shard.shape[0]

    def along_seq(self, *after):
        g = self.grid
        shard = tie(self.shard, *after)
        blocks = [shard] + [g.turn(shard, step) for step in range(1, g.seq)]
        stacked = jnp.stack(blocks[::-1] + blocks[::-1])
        value = lax.dynamic_slice_in_dim(stacked, (g.seq - 1 - g.s) % g.seq, g.seq, 0)
        self.value = value.reshape(1, self.rows, -1)
        return self

    def step(self, *after):
        g, bit = self.grid, self.order[len(self.done)]
        value = tie(self.value, *after)
        other = g.swap(value, bit)
        low = (g.d & bit) == 0
        outer = 1 << sum(1 for have in self.done if have > bit)
        shape = (outer, 1, -1, self.rows, value.shape[-1])
        value, other = value.reshape(shape), other.reshape(shape)
        both = [jnp.where(low, value, other), jnp.where(low, other, value)]
        self.value = jnp.concatenate(both, axis=1).reshape(-1, self.rows, shape[-1])
        self.done.append(bit)
        return self

    def finish(self):
        while len(self.done) < len(self.order):
            self.step()
        return self.value.reshape(-1, self.value.shape[-1])


class Scatter:
    def __init__(self, grid, grad, order):
        self.grid, self.order = grid, [1] + list(order)
        self.left = sorted(self.order, reverse=True)
        self.value, self.arriving = grad, None
        self.rows = grad.shape[0] // (grid.dp * grid.seq)
        self.width = grad.shape[1]
        self.send()

    def send(self):
        g = self.grid
        bit = self.order.pop(0)
        at = self.left.index(bit)
        self.left.remove(bit)
        split = self.value.reshape(1 << at, 2, -1, self.width)
        mine = ((g.d & bit) != 0).astype(jnp.int32)
        self.sent = lax.dynamic_index_in_dim(split, 1 - mine, 1, keepdims=False).astype(bf16)
        self.kept = lax.dynamic_index_in_dim(split, mine, 1, keepdims=False).astype(f32)
        self.arriving = g.swap(self.sent, bit)

    def step(self):
        g = self.grid
        self.value = self.kept + self.arriving.astype(f32)
        if self.order:
            self.send()
            return self.sent
        parts = self.value.reshape(g.seq, self.rows, self.width)
        self.kept = g.pick(parts, g.s)
        steps = range(1, g.seq)
        self.sent = [g.pick(parts, (g.s + k) % g.seq).astype(bf16) for k in steps]
        self.arriving = [g.turn(part, k) for part, k in zip(self.sent, steps)]
        return self.sent[0]

    def finish(self):
        while not isinstance(self.arriving, list):
            self.step()
        return self.kept + sum(part.astype(f32) for part in self.arriving)


def attention_bias(row_ref, col_ref, bias):
    @pl.when(pl.program_id(0) == 0)
    def _():
        bias[...] = jnp.where(col_ref[...] == row_ref[...], 0.0, closed)


def head_lanes(value, head):
    lanes = lax.broadcasted_iota(jnp.int32, value.shape, 1)
    return jnp.where(lanes // HD == head, value, jnp.zeros_like(value))


def attend_kernel(row, col, q, k_own, v_own, k_far, v_far, out, logsum, bias):
    attention_bias(row, col, bias)
    n = q.shape[0]
    turned = []
    v_turned = [v_own[...].T, v_far[...].T]
    for h in range(LANES // HD):
        masked = head_lanes(q[...], h)
        scores = [
            dot(k[...], masked, ((1,), (1,))) + bias[pl.ds(j * n, n), :]
            for j, k in enumerate((k_own, k_far))
        ]
        highest = jnp.maximum(
            jnp.max(scores[0], axis=0, keepdims=True), jnp.max(scores[1], axis=0, keepdims=True)
        )
        expos = [jnp.exp(s - highest) for s in scores]
        totals = sum(jnp.sum(e, axis=0, keepdims=True) for e in expos)
        mixed = sum(
            dot(v[h * HD : (h + 1) * HD], e.astype(bf16), ((1,), (0,)))
            for v, e in zip(v_turned, expos)
        )
        turned.append(mixed / totals)
        logsum[h] = highest + jnp.log(totals)
    out[...] = jnp.concatenate(turned, axis=0).T.astype(bf16)


def attend_back_kernel(
    row, col, q, k_own, v_own, k_far, v_far, attended, grad, logsum,
    dq, dk_own, dv_own, dk_far, dv_far, bias,
):
    attention_bias(row, col, bias)
    n = q.shape[0]
    both = (grad[...].astype(f32) * attended[...].astype(f32)).T
    k_turned = [k_own[...].T, k_far[...].T]
    dq_turned = []
    dks, dvs = [0.0, 0.0], [0.0, 0.0]
    for h in range(LANES // HD):
        masked_q, masked_g = head_lanes(q[...], h), head_lanes(grad[...], h)
        inner = jnp.sum(both[h * HD : (h + 1) * HD], axis=0, keepdims=True)
        dq_head = 0.0
        for j, (k, v) in enumerate(((k_own, v_own), (k_far, v_far))):
            scores = dot(k[...], masked_q, ((1,), (1,))) + bias[pl.ds(j * n, n), :]
            chances = jnp.exp(scores - logsum[h])
            grad_chances = dot(v[...], masked_g, ((1,), (1,)))
            dvs[j] = dvs[j] + dot(chances.astype(bf16), masked_g, ((1,), (0,)))
            grad_scores = (chances * (grad_chances - inner)).astype(bf16)
            dks[j] = dks[j] + dot(grad_scores, masked_q, ((1,), (0,)))
            dq_head = dq_head + dot(
                k_turned[j][h * HD : (h + 1) * HD], grad_scores, ((1,), (0,))
            )
        dq_turned.append(dq_head)
    dq[...] = (jnp.concatenate(dq_turned, axis=0).T * (1.0 / math.sqrt(HD))).astype(dq.dtype)
    for ref, value in ((dk_own, dks[0]), (dv_own, dvs[0]), (dk_far, dks[1]), (dv_far, dvs[1])):
        ref[...] = value.astype(ref.dtype)


def attention_specs(n, width, first):
    def at(offset):
        return pl.BlockSpec((n, LANES), lambda j: (0, offset + first + j))

    row = pl.BlockSpec((1, n), lambda j: (0, 0))
    col = pl.BlockSpec((2 * n, 1), lambda j: (0, 0))
    return [row, col, at(0), at(0), at(width // LANES), at(0), at(width // LANES)], at


def attend(queries, own_kv, far_kv, own_slots, slots):
    n, width = queries.shape
    specs, at = attention_specs(n, width, 0)
    heads = LANES // HD
    return pl.pallas_call(
        attend_kernel,
        grid=(width // LANES,),
        in_specs=specs,
        out_specs=[at(0), pl.BlockSpec((heads, 1, n), lambda j: (j, 0, 0))],
        out_shape=[
            jax.ShapeDtypeStruct((n, width), bf16),
            jax.ShapeDtypeStruct((width // HD, 1, n), f32),
        ],
        scratch_shapes=[pltpu.VMEM((2 * n, n), f32)],
        name="attend",
    )(own_slots[None], slots[:, None], queries, own_kv, own_kv, far_kv, far_kv)


def attend_back(queries, own_kv, far_kv, attended, grad, logsum, own_slots, slots, first, count):
    n, width = queries.shape
    specs, at = attention_specs(n, width, first)
    heads = LANES // HD
    out = pl.BlockSpec((n, LANES), lambda j: (0, j))
    shapes = [jax.ShapeDtypeStruct((n, count * LANES), kind) for kind in (bf16, f32, f32, bf16, bf16)]
    return pl.pallas_call(
        attend_back_kernel,
        grid=(count,),
        in_specs=specs + [at(0), at(0), pl.BlockSpec((heads, 1, n), lambda j: (first + j, 0, 0))],
        out_specs=[out] * 5,
        out_shape=shapes,
        scratch_shapes=[pltpu.VMEM((2 * n, n), f32)],
        name="attend_back",
    )(
        own_slots[None], slots[:, None], queries, own_kv, own_kv, far_kv, far_kv,
        attended, grad, logsum,
    )


def local(
    tokens,
    cotangent,
    lengths,
    gain_one,
    shift_one,
    qkv_weight,
    query_bias,
    value_bias,
    proj_weight,
    proj_bias,
    gain_two,
    shift_two,
    up_weight,
    up_bias,
    down_weight,
    down_bias,
    *,
    dp,
    seq,
):
    micro, block, width = tokens.shape[1:]
    grid = Grid(dp, seq, micro)
    r = qkv_weight.shape[0]
    order_a, order_b = grid.bits, grid.bits[::-1]

    small = [gain_one, shift_one, query_bias, value_bias, proj_bias, gain_two, shift_two, down_bias]
    columns = jnp.concatenate([item.reshape(r, 1) for item in small] + [up_bias.reshape(r, -1)], 1)
    columns = jnp.pad(columns, ((0, 0), (0, LANES - columns.shape[1])))
    packed = jnp.concatenate([qkv_weight, columns], axis=1)
    cut = packed.shape[1] // 2 // LANES * LANES

    qkv_a = Gather(grid, packed[:, :cut], order_a).along_seq()
    qkv_b = Gather(grid, packed[:, cut:], order_b).along_seq()
    inputs = grid.to_packs(tokens[0])
    for _ in grid.bits:
        qkv_a.step()
        qkv_b.step()
    first = (qkv_a.value, qkv_b.value)
    first_half, second_half = qkv_a.finish(), qkv_b.finish()

    columns = second_half[:, 3 * width - cut :].astype(f32)
    rows = columns[:, : len(small)].T
    gain_one_f, shift_one_f, query_b, value_b, proj_b, gain_two_f, shift_two_f, down_b = rows
    up_b = columns[:, len(small) : len(small) + up_bias.shape[0] // r].reshape(-1)
    qkv_w = jnp.concatenate([first_half, second_half[:, : 3 * width - cut]], axis=1)

    proj_g = Gather(grid, proj_weight, order_a).along_seq(inputs)
    up_g = Gather(grid, up_weight, order_a).along_seq(inputs)
    down_g = Gather(grid, down_weight, order_b).along_seq(inputs)
    proj_g.step(*first)
    up_g.step(*first)
    down_g.step(*first)
    grad_out = grid.to_packs(tie(cotangent[0], up_g.value, down_g.value))
    proj_w, up_w, down_w = proj_g.finish(), up_g.finish(), down_g.finish()

    core = grid.d % 2
    away = grid.swap(lengths[0], 1)
    lens = jnp.where(grid.s // micro == core, lengths[0], away)
    lens = grid.pick(lens, grid.s % micro)
    spots = jnp.arange(block, dtype=jnp.int32)
    own_slots = slot_numbers(lens, jnp.concatenate([q * block + spots for q in grid.quarters(core)]))
    far_slots = slot_numbers(
        lens, jnp.concatenate([q * block + spots for q in grid.quarters(1 - core)])
    )
    slots = jnp.concatenate([own_slots, far_slots])

    inputs_f = inputs.astype(f32)
    normed, norm_back = jax.vjp(layer_norm, inputs_f, gain_one_f, shift_one_f)
    first_in = normed.astype(bf16)
    qkv = dot(first_in, qkv_w, ((1,), (0,)))
    queries = (qkv[:, :width] + query_b).astype(bf16) * bf16(1.0 / math.sqrt(HD))
    own_kv = jnp.concatenate(
        [qkv[:, width : 2 * width], qkv[:, 2 * width :] + value_b], axis=1
    ).astype(bf16)
    far_kv = grid.swap(own_kv, 1)
    attended, logsum = attend(queries, own_kv, far_kv, own_slots, slots)

    middle = inputs_f + dot(attended, proj_w, ((1,), (0,))) + proj_b
    second, second_back = jax.vjp(layer_norm, middle, gain_two_f, shift_two_f)
    second_in = second.astype(bf16)
    hidden = dot(second_in, up_w, ((1,), (0,))) + up_b
    share = 0.5 * (1.0 + lax.erf(hidden * math.sqrt(0.5)))
    bell = jnp.exp(-0.5 * hidden * hidden) * (1.0 / math.sqrt(2.0 * math.pi))
    active_in, slope = lax.optimization_barrier(
        ((hidden * share).astype(bf16), (share + hidden * bell).astype(bf16))
    )

    down_s = Scatter(grid, dot(active_in, grad_out, ((0,), (0,))), order_b)
    pull = tie(grad_out, down_s.sent)
    grad_active = dot(pull, down_w, ((1,), (1,)))
    grad_hidden_in = (grad_active * slope.astype(f32)).astype(bf16)
    up_s = Scatter(grid, dot(second_in, grad_hidden_in, ((0,), (0,))), order_a)
    grad_hidden_in = tie(grad_hidden_in, down_s.step(), up_s.sent)
    up_bias_grad = jnp.sum(grad_hidden_in.astype(f32), axis=0)
    grad_second = dot(grad_hidden_in, up_w, ((1,), (1,)))
    grad_float = grad_out.astype(f32)
    down_bias_grad = jnp.sum(grad_float, axis=0)
    grad_middle_part, gain_two_grad, shift_two_grad = second_back(grad_second)
    grad_middle = grad_float + grad_middle_part
    grad_proj = grad_middle.astype(bf16)
    proj_bias_grad = jnp.sum(grad_proj.astype(f32), axis=0)
    grad_attended = dot(grad_proj, proj_w, ((1,), (1,))).astype(bf16)

    output = (middle + dot(active_in, down_w, ((1,), (0,))) + down_b).astype(bf16)
    groups = width // LANES
    grad_attended = tie(grad_attended, up_s.step(), output)
    block_out = grid.from_packs(output)
    pieces = []
    for piece in range(3):
        pieces.append(
            attend_back(
                queries,
                own_kv,
                far_kv,
                attended,
                grad_attended,
                logsum,
                own_slots,
                slots,
                piece * groups // 3,
                groups // 3,
            )
        )
        if piece == 0:
            proj_s = Scatter(grid, dot(attended, grad_proj, ((0,), (0,))), order_a)
            grad_attended = tie(grad_attended, down_s.step(), proj_s.sent, pieces[0][0])
        elif piece == 1:
            grad_attended = tie(grad_attended, up_s.step(), proj_s.step(), pieces[1][0])
    dq, dk, dv, dk_far, dv_far = [jnp.concatenate(part, axis=1) for part in zip(*pieces)]
    dk = dk + grid.swap(dk_far, 1).astype(f32)
    dv = dv + grid.swap(dv_far, 1).astype(f32)
    dqkv = jnp.concatenate([dq, dk.astype(bf16), dv.astype(bf16)], axis=1)
    dqkv = tie(dqkv, down_s.step())
    qkv_grad = dot(first_in, dqkv, ((0,), (0,)))
    qkv_as = Scatter(grid, qkv_grad[:, :cut], order_a)
    qkv_bs = Scatter(grid, qkv_grad[:, cut:], order_b)
    dqkv = tie(dqkv, qkv_as.sent, qkv_bs.sent, up_s.step(), proj_s.step())
    query_bias_grad = jnp.sum(dqkv[:, :width].astype(f32), axis=0)
    value_bias_grad = jnp.sum(dqkv[:, 2 * width :].astype(f32), axis=0)
    grad_first = dot(dqkv, qkv_w, ((1,), (1,)))
    grad_input_part, gain_one_grad, shift_one_grad = norm_back(grad_first)
    input_grad = grid.from_packs((grad_middle + grad_input_part).astype(bf16))

    small_grads = [
        gain_one_grad,
        shift_one_grad,
        query_bias_grad,
        value_bias_grad,
        proj_bias_grad,
        gain_two_grad,
        shift_two_grad,
        down_bias_grad,
    ]
    columns = jnp.concatenate(
        [jnp.stack(small_grads, axis=1), up_bias_grad.reshape(width, -1)], axis=1
    )
    taken = columns.shape[1]
    columns = jnp.pad(columns, ((0, 0), (0, LANES - taken)))
    columns = Scatter(grid, columns, order_a).finish()
    qkv_weight_grad = jnp.concatenate([qkv_as.finish(), qkv_bs.finish()], axis=1)
    (
        gain_one_grad,
        shift_one_grad,
        query_bias_grad,
        value_bias_grad,
        proj_bias_grad,
        gain_two_grad,
        shift_two_grad,
        down_bias_grad,
    ) = [columns[:, j] for j in range(len(small))]
    up_bias_grad = columns[:, len(small) : taken].reshape(-1)
    return (
        block_out[None],
        input_grad[None],
        gain_one_grad,
        shift_one_grad,
        qkv_weight_grad,
        query_bias_grad,
        value_bias_grad,
        proj_s.finish(),
        proj_bias_grad,
        gain_two_grad,
        shift_two_grad,
        up_s.finish(),
        up_bias_grad,
        down_s.finish(),
        down_bias_grad,
    )


def solution(mesh):
    tokens = P("dp", None, "seq", None)
    vector = P(("dp", "seq"))
    matrix = P(("dp", "seq"), None)
    dp, seq = mesh.shape["dp"], mesh.shape["seq"]
    kinds = (
        vector,
        vector,
        matrix,
        vector,
        vector,
        matrix,
        vector,
        vector,
        vector,
        matrix,
        vector,
        matrix,
        vector,
    )
    return jax.shard_map(
        lambda *args: local(*args, dp=dp, seq=seq),
        mesh=mesh,
        in_specs=(tokens, tokens, P("dp", None, None)) + kinds,
        out_specs=(tokens, tokens) + kinds,
        check_vma=False,
    )
```

```python
import math

import jax
import jax.numpy as jnp
from jax import lax
from jax.experimental import pallas as pl
from jax.experimental.pallas import tpu as pltpu
from jax.sharding import PartitionSpec as P

HD = 64
LANES = 128
f32 = jnp.float32
bf16 = jnp.bfloat16

tail_cells = 3
closed = -1e30
norm_eps = 1e-06


def dot(left, right, contract):
    return lax.dot_general(left, right, (contract, ((), ())), preferred_element_type=f32)


def tie(value, *others):
    return lax.optimization_barrier((value,) + others)[0]


def layer_norm(values, gain, shift):
    center = values - jnp.mean(values, axis=-1, keepdims=True)
    spread = jnp.mean(center * center, axis=-1, keepdims=True)
    return center * lax.rsqrt(spread + norm_eps) * gain + shift


def slot_numbers(lens, places):
    widths = jnp.where(lens > 0, lens + tail_cells, 0)
    starts = jnp.cumsum(widths) - widths
    inside = (places[None, :] >= starts[:, None]) & (places[None, :] < (starts + lens)[:, None])
    labels = jnp.arange(lens.shape[0], dtype=jnp.int32) + 1
    return jnp.sum(jnp.where(inside, labels[:, None], 0), axis=0) - 1


class Grid:
    def __init__(self, dp, seq, micro):
        assert dp & (dp - 1) == 0 and seq == 2 * micro
        self.dp, self.seq, self.micro = dp, seq, micro
        self.bits = [1 << k for k in range(1, dp.bit_length() - 1)]
        self.d = lax.axis_index("dp")
        self.s = lax.axis_index("seq")

    def swap(self, value, bit):
        return lax.ppermute(value, "dp", [(k, k ^ bit) for k in range(self.dp)])

    def turn(self, value, step):
        return lax.ppermute(value, "seq", [(k, (k + step) % self.seq) for k in range(self.seq)])

    def routes(self):
        found = []
        half = self.seq // 2
        for p in range(self.micro):
            pairs = []
            for c in range(self.dp // 2):
                for a in range(2):
                    for s in range(self.seq):
                        m = (s + p) % self.micro
                        k, z = s // half, a * self.micro + m
                        pairs.append(((2 * c + a) * self.seq + s, (2 * c + k) * self.seq + z))
            found.append(pairs)
        return found

    def pick(self, blocks, index):
        return lax.dynamic_index_in_dim(blocks, index, 0, keepdims=False)

    def to_packs(self, blocks, *late):
        got = [
            lax.ppermute(self.pick(blocks, (self.s + p) % self.micro), ("dp", "seq"), pairs)
            for p, pairs in enumerate(self.routes())
        ]
        return jnp.concatenate([tie(part, *late) for part in got], axis=0)

    def from_packs(self, rows, *late):
        parts = rows.reshape(self.micro, -1, rows.shape[-1])
        got = [
            lax.ppermute(parts[p], ("dp", "seq"), [(b, a) for a, b in pairs])
            for p, pairs in enumerate(self.routes())
        ]
        got = jnp.stack([tie(part, *late) for part in got])
        return jnp.roll(got, self.s % self.micro, axis=0)

    def quarters(self, core):
        own = self.s % self.micro
        half = self.seq // 2
        return [half * core + (own - p) % self.micro for p in range(self.micro)]


class Gather:
    def __init__(self, grid, shard, streams, after=(), late=()):
        self.grid, self.rows = grid, grid.seq * shard.shape[0]
        shard = tie(shard, *after)
        blocks = [shard]
        blocks += [tie(grid.turn(shard, step), *late) for step in range(1, grid.seq)]
        self.streams = []
        start = 0
        for width, order in streams:
            parts = [block[:, start : start + width] for block in blocks]
            stacked = jnp.stack(parts[::-1] + parts[::-1])
            value = lax.dynamic_slice_in_dim(
                stacked, (grid.seq - 1 - grid.s) % grid.seq, grid.seq, 0
            )
            self.streams.append([value.reshape(1, self.rows, width), list(order) + [1], []])
            start += width

    def step(self, *late):
        for stream in self.streams:
            self.move(stream, *late)

    def move(self, stream, *late):
        g = self.grid
        value, order, done = stream
        bit = order.pop(0)
        other = tie(g.swap(value, bit), *late)
        low = (g.d & bit) == 0
        outer = 1 << sum(1 for have in done if have > bit)
        shape = (outer, 1, -1, self.rows, value.shape[-1])
        value, other = value.reshape(shape), other.reshape(shape)
        both = [jnp.where(low, value, other), jnp.where(low, other, value)]
        stream[0] = jnp.concatenate(both, axis=1).reshape(-1, self.rows, shape[-1])
        done.append(bit)

    def values(self):
        return [stream[0] for stream in self.streams]

    def finish(self, *late):
        while self.streams[0][1]:
            self.step(*late)
        return [value.reshape(-1, value.shape[-1]) for value in self.values()]


class Scatter:
    def __init__(self, grid, grad, order):
        self.grid, self.order = grid, [1] + list(order)
        self.left = sorted(self.order, reverse=True)
        self.value = grad
        self.rows = grad.shape[0] // (grid.dp * grid.seq)
        self.width = grad.shape[1]
        self.send()

    def send(self):
        g = self.grid
        bit = self.order.pop(0)
        at = self.left.index(bit)
        self.left.remove(bit)
        split = self.value.reshape(1 << at, 2, -1, self.width)
        mine = ((g.d & bit) != 0).astype(jnp.int32)
        self.sent = lax.dynamic_index_in_dim(split, 1 - mine, 1, keepdims=False).astype(bf16)
        self.kept = lax.dynamic_index_in_dim(split, mine, 1, keepdims=False)
        self.arriving = g.swap(self.sent, bit)

    def step(self):
        self.value = self.kept.astype(f32) + self.arriving.astype(f32)
        if self.order:
            self.send()
            return self.sent
        self.value = self.value.reshape(self.grid.seq, self.rows, self.width)
        return None

    def last(self):
        while self.step() is not None:
            pass
        return self.value


class Along:
    def __init__(self, grid, parts):
        self.own = grid.pick(parts, grid.s).astype(f32)
        steps = range(1, grid.seq)
        self.sent = [grid.pick(parts, (grid.s + step) % grid.seq).astype(bf16) for step in steps]
        self.got = [grid.turn(part, step) for part, step in zip(self.sent, steps)]

    def finish(self, *late):
        return self.own + sum(tie(part, *late).astype(f32) for part in self.got)


def attention_bias(row_ref, col_ref, bias):
    @pl.when(pl.program_id(0) == 0)
    def _():
        bias[...] = jnp.where(col_ref[...] == row_ref[...], 0.0, closed)


def head_lanes(value, head):
    lanes = lax.broadcasted_iota(jnp.int32, value.shape, 1)
    return jnp.where(lanes // HD == head, value, jnp.zeros_like(value))


def attend_kernel(row, col, q, k_own, v_own, k_far, v_far, out, logsum, bias):
    attention_bias(row, col, bias)
    n = q.shape[0]
    turned = []
    v_turned = [v_own[...].T, v_far[...].T]
    for h in range(LANES // HD):
        masked = head_lanes(q[...], h)
        scores = [
            dot(k[...], masked, ((1,), (1,))) + bias[pl.ds(j * n, n), :]
            for j, k in enumerate((k_own, k_far))
        ]
        highest = jnp.maximum(
            jnp.max(scores[0], axis=0, keepdims=True), jnp.max(scores[1], axis=0, keepdims=True)
        )
        expos = [jnp.exp(s - highest) for s in scores]
        totals = sum(jnp.sum(e, axis=0, keepdims=True) for e in expos)
        mixed = sum(
            dot(v[h * HD : (h + 1) * HD], e.astype(bf16), ((1,), (0,)))
            for v, e in zip(v_turned, expos)
        )
        turned.append(mixed / totals)
        logsum[h] = highest + jnp.log(totals)
    out[...] = jnp.concatenate(turned, axis=0).T.astype(bf16)


def attend_back_kernel(
    row, col, q, k_own, v_own, k_far, v_far, attended, grad, logsum,
    *rest,
):
    dq, own, far, bias = rest[-4:]
    attention_bias(row, col, bias)
    n = q.shape[0]
    both = (grad[...].astype(f32) * attended[...].astype(f32)).T
    k_turned = [k_own[...].T, k_far[...].T]
    dq_turned = []
    dks, dvs = [0.0, 0.0], [0.0, 0.0]
    for h in range(LANES // HD):
        masked_q, masked_g = head_lanes(q[...], h), head_lanes(grad[...], h)
        inner = jnp.sum(both[h * HD : (h + 1) * HD], axis=0, keepdims=True)
        dq_head = 0.0
        for j, (k, v) in enumerate(((k_own, v_own), (k_far, v_far))):
            scores = dot(k[...], masked_q, ((1,), (1,))) + bias[pl.ds(j * n, n), :]
            chances = jnp.exp(scores - logsum[h])
            grad_chances = dot(v[...], masked_g, ((1,), (1,)))
            dvs[j] = dvs[j] + dot(chances.astype(bf16), masked_g, ((1,), (0,)))
            grad_scores = (chances * (grad_chances - inner)).astype(bf16)
            dks[j] = dks[j] + dot(grad_scores, masked_q, ((1,), (0,)))
            dq_head = dq_head + dot(
                k_turned[j][h * HD : (h + 1) * HD], grad_scores, ((1,), (0,))
            )
        dq_turned.append(dq_head)
    dq[...] = (jnp.concatenate(dq_turned, axis=0).T * (1.0 / math.sqrt(HD))).astype(dq.dtype)
    own[0], own[1] = dks[0], dvs[0]
    far[0], far[1] = dks[1].astype(far.dtype), dvs[1].astype(far.dtype)


def attention_specs(n, width, first):
    def at(offset):
        return pl.BlockSpec((n, LANES), lambda j: (0, offset + first + j))

    row = pl.BlockSpec((1, n), lambda j: (0, 0))
    col = pl.BlockSpec((2 * n, 1), lambda j: (0, 0))
    return [row, col, at(0), at(0), at(width // LANES), at(0), at(width // LANES)], at


def attend(queries, own_kv, far_kv, own_slots, slots):
    n, width = queries.shape
    specs, at = attention_specs(n, width, 0)
    heads = LANES // HD
    return pl.pallas_call(
        attend_kernel,
        grid=(width // LANES,),
        in_specs=specs,
        out_specs=[at(0), pl.BlockSpec((heads, 1, n), lambda j: (j, 0, 0))],
        out_shape=[
            jax.ShapeDtypeStruct((n, width), bf16),
            jax.ShapeDtypeStruct((width // HD, 1, n), f32),
        ],
        scratch_shapes=[pltpu.VMEM((2 * n, n), f32)],
        name="attend",
    )(own_slots[None], slots[:, None], queries, own_kv, own_kv, far_kv, far_kv)


def attend_back(queries, own_kv, far_kv, attended, grad, logsum, own_slots, slots, before, first, count):
    n, width = queries.shape
    specs, at = attention_specs(n, width, first)
    heads = LANES // HD
    pair = pl.BlockSpec((2, n, LANES), lambda j: (0, 0, first + j))
    before = () if before is None else before
    return pl.pallas_call(
        attend_back_kernel,
        grid=(count,),
        in_specs=specs
        + [at(0), at(0), pl.BlockSpec((heads, 1, n), lambda j: (first + j, 0, 0))]
        + [pl.BlockSpec(memory_space=pl.ANY)] * len(before),
        out_specs=[at(0), pair, pair],
        out_shape=[
            jax.ShapeDtypeStruct((n, width), bf16),
            jax.ShapeDtypeStruct((2, n, width), f32),
            jax.ShapeDtypeStruct((2, n, width), bf16),
        ],
        input_output_aliases={10 + j: j for j in range(len(before))},
        scratch_shapes=[pltpu.VMEM((2 * n, n), f32)],
        name="attend_back",
    )(
        own_slots[None],
        slots[:, None],
        queries,
        own_kv,
        own_kv,
        far_kv,
        far_kv,
        attended,
        grad,
        logsum,
        *before,
    )


def local(
    tokens,
    cotangent,
    lengths,
    gain_one,
    shift_one,
    qkv_weight,
    query_bias,
    value_bias,
    proj_weight,
    proj_bias,
    gain_two,
    shift_two,
    up_weight,
    up_bias,
    down_weight,
    down_bias,
    *,
    dp,
    seq,
):
    micro, block, width = tokens.shape[1:]
    grid = Grid(dp, seq, micro)
    r = qkv_weight.shape[0]
    order_a, order_b = grid.bits, grid.bits[::-1]

    small = [gain_one, shift_one, query_bias, value_bias, proj_bias, gain_two, shift_two, down_bias]
    columns = jnp.concatenate([item.reshape(r, 1) for item in small] + [up_bias.reshape(r, -1)], 1)
    columns = jnp.pad(columns, ((0, 0), (0, LANES - columns.shape[1])))
    packed = jnp.concatenate([qkv_weight, columns], axis=1)
    cut = packed.shape[1] // 2 // LANES * LANES

    qkv_g = Gather(grid, packed, ((cut, order_a), (packed.shape[1] - cut, order_b)))
    inputs = grid.to_packs(tokens[0])
    for _ in grid.bits:
        qkv_g.step()
    first_half, second_half = qkv_g.finish()

    hidden_width = up_weight.shape[1]
    head_values = qkv_g.values()
    up_g = Gather(
        grid,
        jnp.concatenate([up_weight, proj_weight], axis=1),
        ((hidden_width + width, order_a),),
        (inputs,),
        head_values,
    )
    down_g = Gather(grid, down_weight, ((width, order_b),), (inputs,), head_values)

    columns = second_half[:, 3 * width - cut :].astype(f32)
    rows = columns[:, : len(small)].T
    gain_one_f, shift_one_f, query_b, value_b, proj_b, gain_two_f, shift_two_f, down_b = rows
    up_b = columns[:, len(small) : len(small) + up_bias.shape[0] // r].reshape(-1)
    qkv_w = jnp.concatenate([first_half, second_half[:, : 3 * width - cut]], axis=1)

    core = grid.d % 2
    away = grid.swap(lengths[0], 1)
    lens = jnp.where(grid.s // micro == core, lengths[0], away)
    lens = grid.pick(lens, grid.s % micro)
    spots = jnp.arange(block, dtype=jnp.int32)
    own_slots = slot_numbers(lens, jnp.concatenate([q * block + spots for q in grid.quarters(core)]))
    far_slots = slot_numbers(
        lens, jnp.concatenate([q * block + spots for q in grid.quarters(1 - core)])
    )
    slots = jnp.concatenate([own_slots, far_slots])

    inputs_f = inputs.astype(f32)
    normed, norm_back = jax.vjp(layer_norm, inputs_f, gain_one_f, shift_one_f)
    first_in = normed.astype(bf16)
    qkv = dot(first_in, qkv_w, ((1,), (0,)))
    queries = (qkv[:, :width] + query_b).astype(bf16) * bf16(1.0 / math.sqrt(HD))
    own_kv = jnp.concatenate(
        [qkv[:, width : 2 * width], qkv[:, 2 * width :] + value_b], axis=1
    ).astype(bf16)
    far_kv = grid.swap(own_kv, 1)
    up_g.step(own_kv)
    down_g.step(own_kv)
    sent = up_g.values() + down_g.values()
    attended, logsum = attend(tie(queries, *sent), own_kv, far_kv, own_slots, slots)
    grad_out = grid.to_packs(tie(cotangent[0], own_kv), attended)
    (up_proj,) = up_g.finish(attended)
    (down_w,) = down_g.finish(attended)
    up_w, proj_w = up_proj[:, :hidden_width], up_proj[:, hidden_width:]

    middle = inputs_f + dot(attended, proj_w, ((1,), (0,))) + proj_b
    second, second_back = jax.vjp(layer_norm, middle, gain_two_f, shift_two_f)
    second_in = second.astype(bf16)
    hidden = dot(second_in, up_w, ((1,), (0,))) + up_b
    share = 0.5 * (1.0 + lax.erf(hidden * math.sqrt(0.5)))
    bell = jnp.exp(-0.5 * hidden * hidden) * (1.0 / math.sqrt(2.0 * math.pi))
    active_in, slope = lax.optimization_barrier(
        ((hidden * share).astype(bf16), (share + hidden * bell).astype(bf16))
    )

    down_s = Scatter(grid, dot(active_in, grad_out, ((0,), (0,))).astype(bf16), order_b)
    pull = tie(grad_out, down_s.sent)
    grad_active = dot(pull, down_w, ((1,), (1,)))
    grad_hidden_in = (grad_active * slope.astype(f32)).astype(bf16)
    up_s = Scatter(grid, dot(second_in, grad_hidden_in, ((0,), (0,))).astype(bf16), order_a)
    grad_hidden_in = tie(grad_hidden_in, down_s.step(), up_s.sent)
    up_bias_grad = jnp.sum(grad_hidden_in.astype(f32), axis=0)
    grad_second = dot(grad_hidden_in, up_w, ((1,), (1,)))
    grad_float = grad_out.astype(f32)
    down_bias_grad = jnp.sum(grad_float, axis=0)
    grad_middle_part, gain_two_grad, shift_two_grad = second_back(grad_second)
    grad_middle = grad_float + grad_middle_part
    grad_proj = grad_middle.astype(bf16)
    proj_bias_grad = jnp.sum(grad_proj.astype(f32), axis=0)
    grad_attended = dot(grad_proj, proj_w, ((1,), (1,))).astype(bf16)

    output = (middle + dot(active_in, down_w, ((1,), (0,))) + down_b).astype(bf16)
    groups = width // LANES
    grad_attended = tie(grad_attended, up_s.step(), output)
    grads = None
    for piece in range(3):
        grads = attend_back(
            queries,
            own_kv,
            far_kv,
            attended,
            grad_attended,
            logsum,
            own_slots,
            slots,
            grads,
            piece * groups // 3,
            groups // 3,
        )
        if piece == 0:
            grad_attended = tie(grad_attended, down_s.step(), grads[0])
        elif piece == 1:
            grad_attended = tie(grad_attended, up_s.step(), grads[0])
    dq, own, far = grads
    block_out = grid.from_packs(output, dq)
    far = grid.swap(far, 1)
    down_z = Along(grid, down_s.last())
    proj_grad = dot(tie(attended, dq), grad_proj, ((0,), (0,))).astype(bf16)
    both = (own + far.astype(f32)).astype(bf16)
    dqkv = jnp.concatenate([dq, both[0], both[1]], axis=1)
    dqkv = tie(dqkv, *down_z.sent)
    split = 2 * width
    qk_s = Scatter(grid, dot(first_in, dqkv[:, :split], ((0,), (0,))).astype(bf16), order_a)
    v_grad = dot(first_in, dqkv[:, split:], ((0,), (0,))).astype(bf16)
    up_z = Along(grid, up_s.last())
    dqkv = tie(dqkv, qk_s.sent, *up_z.sent)
    query_bias_grad = jnp.sum(dqkv[:, :width].astype(f32), axis=0)
    value_bias_grad = jnp.sum(dqkv[:, split:].astype(f32), axis=0)
    grad_first = dot(dqkv, qkv_w, ((1,), (1,)))
    grad_input_part, gain_one_grad, shift_one_grad = norm_back(grad_first)
    input_grad = (grad_middle + grad_input_part).astype(bf16)

    small_grads = [
        gain_one_grad,
        shift_one_grad,
        query_bias_grad,
        value_bias_grad,
        proj_bias_grad,
        gain_two_grad,
        shift_two_grad,
        down_bias_grad,
    ]
    columns = jnp.concatenate(
        [jnp.stack(small_grads, axis=1), up_bias_grad.reshape(width, -1)], axis=1
    )
    taken = columns.shape[1]
    columns = jnp.pad(columns, ((0, 0), (0, LANES - taken)))
    v_s = Scatter(grid, jnp.concatenate([v_grad, proj_grad, columns.astype(bf16)], axis=1), order_b)
    input_grad = grid.from_packs(tie(input_grad, v_s.sent))
    late = (qk_s.step(), v_s.step())
    down_weight_grad, up_weight_grad = down_z.finish(*late), up_z.finish(*late)
    packed = jnp.concatenate([qk_s.last(), v_s.last()], axis=2)
    packed = Along(grid, packed).finish()
    qkv_weight_grad, proj_weight_grad = packed[:, : 3 * width], packed[:, 3 * width : 4 * width]
    columns = packed[:, 4 * width :]
    (
        gain_one_grad,
        shift_one_grad,
        query_bias_grad,
        value_bias_grad,
        proj_bias_grad,
        gain_two_grad,
        shift_two_grad,
        down_bias_grad,
    ) = [columns[:, j] for j in range(len(small))]
    up_bias_grad = columns[:, len(small) : taken].reshape(-1)
    return (
        block_out[None],
        input_grad[None],
        gain_one_grad,
        shift_one_grad,
        qkv_weight_grad,
        query_bias_grad,
        value_bias_grad,
        proj_weight_grad,
        proj_bias_grad,
        gain_two_grad,
        shift_two_grad,
        up_weight_grad,
        up_bias_grad,
        down_weight_grad,
        down_bias_grad,
    )


def solution(mesh):
    tokens = P("dp", None, "seq", None)
    vector = P(("dp", "seq"))
    matrix = P(("dp", "seq"), None)
    dp, seq = mesh.shape["dp"], mesh.shape["seq"]
    kinds = (
        vector,
        vector,
        matrix,
        vector,
        vector,
        matrix,
        vector,
        vector,
        vector,
        matrix,
        vector,
        matrix,
        vector,
    )
    return jax.shard_map(
        lambda *args: local(*args, dp=dp, seq=seq),
        mesh=mesh,
        in_specs=(tokens, tokens, P("dp", None, None)) + kinds,
        out_specs=(tokens, tokens) + kinds,
        check_vma=False,
    )
```

```python
import math

import jax
import jax.numpy as jnp
from jax import lax
from jax.experimental import pallas as pl
from jax.experimental.pallas import tpu as pltpu
from jax.sharding import PartitionSpec as P

HD = 64
LANES = 128
f32 = jnp.float32
bf16 = jnp.bfloat16

tail_cells = 3
closed = -1e30
norm_eps = 1e-06


def dot(left, right, contract):
    return lax.dot_general(left, right, (contract, ((), ())), preferred_element_type=f32)


def tie(value, *others):
    return lax.optimization_barrier((value,) + others)[0]


def layer_norm(values, gain, shift):
    center = values - jnp.mean(values, axis=-1, keepdims=True)
    spread = jnp.mean(center * center, axis=-1, keepdims=True)
    return center * lax.rsqrt(spread + norm_eps) * gain + shift


def slot_numbers(lens, places):
    widths = jnp.where(lens > 0, lens + tail_cells, 0)
    starts = jnp.cumsum(widths) - widths
    inside = (places[None, :] >= starts[:, None]) & (places[None, :] < (starts + lens)[:, None])
    labels = jnp.arange(lens.shape[0], dtype=jnp.int32) + 1
    return jnp.sum(jnp.where(inside, labels[:, None], 0), axis=0) - 1


class Grid:
    def __init__(self, dp, seq, micro):
        assert dp & (dp - 1) == 0 and seq == 2 * micro
        self.dp, self.seq, self.micro = dp, seq, micro
        self.bits = [1 << k for k in range(1, dp.bit_length() - 1)]
        self.d = lax.axis_index("dp")
        self.s = lax.axis_index("seq")

    def swap(self, value, bit):
        return lax.ppermute(value, "dp", [(k, k ^ bit) for k in range(self.dp)])

    def turn(self, value, step):
        return lax.ppermute(value, "seq", [(k, (k + step) % self.seq) for k in range(self.seq)])

    def routes(self):
        found = []
        half = self.seq // 2
        for p in range(self.micro):
            pairs = []
            for c in range(self.dp // 2):
                for a in range(2):
                    for s in range(self.seq):
                        m = (s + p) % self.micro
                        k, z = s // half, a * self.micro + m
                        pairs.append(((2 * c + a) * self.seq + s, (2 * c + k) * self.seq + z))
            found.append(pairs)
        return found

    def pick(self, blocks, index):
        return lax.dynamic_index_in_dim(blocks, index, 0, keepdims=False)

    def to_packs(self, blocks, *late):
        got = [
            lax.ppermute(self.pick(blocks, (self.s + p) % self.micro), ("dp", "seq"), pairs)
            for p, pairs in enumerate(self.routes())
        ]
        return jnp.concatenate([tie(part, *late) for part in got], axis=0)

    def from_packs(self, rows, *late):
        parts = rows.reshape(self.micro, -1, rows.shape[-1])
        got = [
            lax.ppermute(parts[p], ("dp", "seq"), [(b, a) for a, b in pairs])
            for p, pairs in enumerate(self.routes())
        ]
        got = jnp.stack([tie(part, *late) for part in got])
        return jnp.roll(got, self.s % self.micro, axis=0)

    def quarters(self, core):
        own = self.s % self.micro
        half = self.seq // 2
        return [half * core + (own - p) % self.micro for p in range(self.micro)]


class Gather:
    def __init__(self, grid, shard, streams, after=(), late=()):
        self.grid, self.rows = grid, grid.seq * shard.shape[0]
        shard = tie(shard, *after)
        blocks = [shard]
        blocks += [tie(grid.turn(shard, step), *late) for step in range(1, grid.seq)]
        self.streams = []
        start = 0
        for width, order in streams:
            parts = [block[:, start : start + width] for block in blocks]
            stacked = jnp.stack(parts[::-1] + parts[::-1])
            value = lax.dynamic_slice_in_dim(
                stacked, (grid.seq - 1 - grid.s) % grid.seq, grid.seq, 0
            )
            self.streams.append([value.reshape(1, self.rows, width), list(order) + [1], []])
            start += width

    def step(self, *late):
        for stream in self.streams:
            self.move(stream, *late)

    def move(self, stream, *late):
        g = self.grid
        value, order, done = stream
        bit = order.pop(0)
        other = tie(g.swap(value, bit), *late)
        low = (g.d & bit) == 0
        outer = 1 << sum(1 for have in done if have > bit)
        shape = (outer, 1, -1, self.rows, value.shape[-1])
        value, other = value.reshape(shape), other.reshape(shape)
        both = [jnp.where(low, value, other), jnp.where(low, other, value)]
        stream[0] = jnp.concatenate(both, axis=1).reshape(-1, self.rows, shape[-1])
        done.append(bit)

    def values(self):
        return [stream[0] for stream in self.streams]

    def finish(self, *late):
        while self.streams[0][1]:
            self.step(*late)
        return [value.reshape(-1, value.shape[-1]) for value in self.values()]


class Scatter:
    def __init__(self, grid, grad, order):
        self.grid, self.order = grid, [1] + list(order)
        self.left = sorted(self.order, reverse=True)
        self.value = grad
        self.rows = grad.shape[0] // (grid.dp * grid.seq)
        self.width = grad.shape[1]
        self.send()

    def send(self):
        g = self.grid
        bit = self.order.pop(0)
        at = self.left.index(bit)
        self.left.remove(bit)
        split = self.value.reshape(1 << at, 2, -1, self.width)
        mine = ((g.d & bit) != 0).astype(jnp.int32)
        self.sent = lax.dynamic_index_in_dim(split, 1 - mine, 1, keepdims=False).astype(bf16)
        self.kept = lax.dynamic_index_in_dim(split, mine, 1, keepdims=False)
        self.arriving = g.swap(self.sent, bit)

    def step(self):
        self.value = self.kept.astype(f32) + self.arriving.astype(f32)
        if self.order:
            self.send()
            return self.sent
        self.value = self.value.reshape(self.grid.seq, self.rows, self.width)
        return None

    def last(self):
        while self.step() is not None:
            pass
        return self.value


class Along:
    def __init__(self, grid, parts):
        self.own = grid.pick(parts, grid.s).astype(f32)
        steps = range(1, grid.seq)
        self.sent = [grid.pick(parts, (grid.s + step) % grid.seq).astype(bf16) for step in steps]
        self.got = [grid.turn(part, step) for part, step in zip(self.sent, steps)]

    def finish(self, *late):
        return self.own + sum(tie(part, *late).astype(f32) for part in self.got)


def attention_bias(row_ref, col_ref, bias):
    @pl.when(pl.program_id(0) == 0)
    def _():
        bias[...] = jnp.where(col_ref[...] == row_ref[...], 0.0, closed)


def head_lanes(value, head):
    lanes = lax.broadcasted_iota(jnp.int32, value.shape, 1)
    return jnp.where(lanes // HD == head, value, jnp.zeros_like(value))


def attend_kernel(row, col, q, k_own, v_own, k_far, v_far, out, logsum, bias):
    attention_bias(row, col, bias)
    n = q.shape[0]
    turned = []
    v_turned = [v_own[...].T, v_far[...].T]
    for h in range(LANES // HD):
        masked = head_lanes(q[...], h)
        scores = [
            dot(k[...], masked, ((1,), (1,))) + bias[pl.ds(j * n, n), :]
            for j, k in enumerate((k_own, k_far))
        ]
        highest = jnp.maximum(
            jnp.max(scores[0], axis=0, keepdims=True), jnp.max(scores[1], axis=0, keepdims=True)
        )
        expos = [jnp.exp(s - highest) for s in scores]
        totals = sum(jnp.sum(e, axis=0, keepdims=True) for e in expos)
        mixed = sum(
            dot(v[h * HD : (h + 1) * HD], e.astype(bf16), ((1,), (0,)))
            for v, e in zip(v_turned, expos)
        )
        turned.append(mixed / totals)
        logsum[h] = highest + jnp.log(totals)
    out[...] = jnp.concatenate(turned, axis=0).T.astype(bf16)


def attend_back_kernel(
    row, col, q, k_own, v_own, k_far, v_far, attended, grad, logsum,
    dq, own, far, bias,
):
    attention_bias(row, col, bias)
    n = q.shape[0]
    both = (grad[...].astype(f32) * attended[...].astype(f32)).T
    k_turned = [k_own[...].T, k_far[...].T]
    dq_turned = []
    dks, dvs = [0.0, 0.0], [0.0, 0.0]
    for h in range(LANES // HD):
        masked_q, masked_g = head_lanes(q[...], h), head_lanes(grad[...], h)
        inner = jnp.sum(both[h * HD : (h + 1) * HD], axis=0, keepdims=True)
        dq_head = 0.0
        for j, (k, v) in enumerate(((k_own, v_own), (k_far, v_far))):
            scores = dot(k[...], masked_q, ((1,), (1,))) + bias[pl.ds(j * n, n), :]
            chances = jnp.exp(scores - logsum[h])
            grad_chances = dot(v[...], masked_g, ((1,), (1,)))
            dvs[j] = dvs[j] + dot(chances.astype(bf16), masked_g, ((1,), (0,)))
            grad_scores = (chances * (grad_chances - inner)).astype(bf16)
            dks[j] = dks[j] + dot(grad_scores, masked_q, ((1,), (0,)))
            dq_head = dq_head + dot(
                k_turned[j][h * HD : (h + 1) * HD], grad_scores, ((1,), (0,))
            )
        dq_turned.append(dq_head)
    dq[...] = (jnp.concatenate(dq_turned, axis=0).T * (1.0 / math.sqrt(HD))).astype(dq.dtype)
    own[0], own[1] = dks[0], dvs[0]
    far[0], far[1] = dks[1].astype(far.dtype), dvs[1].astype(far.dtype)


def attention_specs(n, width):
    def at(offset):
        return pl.BlockSpec((n, LANES), lambda j: (0, offset + j))

    row = pl.BlockSpec((1, n), lambda j: (0, 0))
    col = pl.BlockSpec((2 * n, 1), lambda j: (0, 0))
    return [row, col, at(0), at(0), at(width // LANES), at(0), at(width // LANES)], at


def attend(queries, own_kv, far_kv, own_slots, slots):
    n, width = queries.shape
    specs, at = attention_specs(n, width)
    heads = LANES // HD
    return pl.pallas_call(
        attend_kernel,
        grid=(width // LANES,),
        in_specs=specs,
        out_specs=[at(0), pl.BlockSpec((heads, 1, n), lambda j: (j, 0, 0))],
        out_shape=[
            jax.ShapeDtypeStruct((n, width), bf16),
            jax.ShapeDtypeStruct((width // HD, 1, n), f32),
        ],
        scratch_shapes=[pltpu.VMEM((2 * n, n), f32)],
        name="attend",
    )(own_slots[None], slots[:, None], queries, own_kv, own_kv, far_kv, far_kv)


def attend_back(queries, own_kv, far_kv, attended, grad, logsum, own_slots, slots):
    n, width = queries.shape
    specs, at = attention_specs(n, width)
    heads = LANES // HD
    pair = pl.BlockSpec((2, n, LANES), lambda j: (0, 0, j))
    return pl.pallas_call(
        attend_back_kernel,
        grid=(width // LANES,),
        in_specs=specs
        + [at(0), at(0), pl.BlockSpec((heads, 1, n), lambda j: (j, 0, 0))],
        out_specs=[at(0), pair, pair],
        out_shape=[
            jax.ShapeDtypeStruct((n, width), bf16),
            jax.ShapeDtypeStruct((2, n, width), f32),
            jax.ShapeDtypeStruct((2, n, width), bf16),
        ],
        scratch_shapes=[pltpu.VMEM((2 * n, n), f32)],
        name="attend_back",
    )(
        own_slots[None],
        slots[:, None],
        queries,
        own_kv,
        own_kv,
        far_kv,
        far_kv,
        attended,
        grad,
        logsum,
    )


def local(
    tokens,
    cotangent,
    lengths,
    gain_one,
    shift_one,
    qkv_weight,
    query_bias,
    value_bias,
    proj_weight,
    proj_bias,
    gain_two,
    shift_two,
    up_weight,
    up_bias,
    down_weight,
    down_bias,
    *,
    dp,
    seq,
):
    micro, block, width = tokens.shape[1:]
    grid = Grid(dp, seq, micro)
    r = qkv_weight.shape[0]
    order_a, order_b = grid.bits, grid.bits[::-1]

    small = [gain_one, shift_one, query_bias, value_bias, proj_bias, gain_two, shift_two, down_bias]
    columns = jnp.concatenate([item.reshape(r, 1) for item in small] + [up_bias.reshape(r, -1)], 1)
    columns = jnp.pad(columns, ((0, 0), (0, LANES - columns.shape[1])))
    packed = jnp.concatenate([qkv_weight, columns], axis=1)
    cut = packed.shape[1] // 2 // LANES * LANES

    qkv_g = Gather(grid, packed, ((cut, order_a), (packed.shape[1] - cut, order_b)))
    inputs = grid.to_packs(tokens[0])
    for _ in grid.bits:
        qkv_g.step()
    first_half, second_half = qkv_g.finish()

    n, hidden_width = dp * seq, up_weight.shape[1]
    q = hidden_width // width
    up_rows = up_weight.reshape(r, q, width).transpose(1, 0, 2).reshape(q * r, width)
    others = lax.all_gather(
        jnp.concatenate([up_rows, proj_weight, down_weight], axis=0), ("dp", "seq"), axis=0, tiled=False
    )

    columns = second_half[:, 3 * width - cut :].astype(f32)
    rows = columns[:, : len(small)].T
    gain_one_f, shift_one_f, query_b, value_b, proj_b, gain_two_f, shift_two_f, down_b = rows
    up_b = columns[:, len(small) : len(small) + up_bias.shape[0] // r].reshape(-1)
    qkv_w = jnp.concatenate([first_half, second_half[:, : 3 * width - cut]], axis=1)

    core = grid.d % 2
    away = grid.swap(lengths[0], 1)
    lens = jnp.where(grid.s // micro == core, lengths[0], away)
    lens = grid.pick(lens, grid.s % micro)
    spots = jnp.arange(block, dtype=jnp.int32)
    own_slots = slot_numbers(lens, jnp.concatenate([q * block + spots for q in grid.quarters(core)]))
    far_slots = slot_numbers(
        lens, jnp.concatenate([q * block + spots for q in grid.quarters(1 - core)])
    )
    slots = jnp.concatenate([own_slots, far_slots])

    inputs_f = inputs.astype(f32)
    normed, norm_back = jax.vjp(layer_norm, inputs_f, gain_one_f, shift_one_f)
    first_in = normed.astype(bf16)
    qkv = dot(first_in, qkv_w, ((1,), (0,)))
    queries = (qkv[:, :width] + query_b).astype(bf16) * bf16(1.0 / math.sqrt(HD))
    own_kv = jnp.concatenate(
        [qkv[:, width : 2 * width], qkv[:, 2 * width :] + value_b], axis=1
    ).astype(bf16)
    far_kv = grid.swap(own_kv, 1)
    attended, logsum = attend(queries, own_kv, far_kv, own_slots, slots)
    grad_out = grid.to_packs(tie(cotangent[0], own_kv), attended)
    others = tie(others, attended)
    up_w = others[:, : q * r].reshape(n, q, r, width).transpose(0, 2, 1, 3).reshape(width, -1)
    proj_w = others[:, q * r : q * r + r].reshape(width, width)
    down_w = others[:, q * r + r :].reshape(hidden_width, width)

    middle = inputs_f + dot(attended, proj_w, ((1,), (0,))) + proj_b
    second, second_back = jax.vjp(layer_norm, middle, gain_two_f, shift_two_f)
    second_in = second.astype(bf16)
    hidden = dot(second_in, up_w, ((1,), (0,))) + up_b
    share = 0.5 * (1.0 + lax.erf(hidden * math.sqrt(0.5)))
    bell = jnp.exp(-0.5 * hidden * hidden) * (1.0 / math.sqrt(2.0 * math.pi))
    active_in, slope = lax.optimization_barrier(
        ((hidden * share).astype(bf16), (share + hidden * bell).astype(bf16))
    )

    down_grad = dot(active_in, grad_out, ((0,), (0,))).astype(bf16).reshape(n, q * r, width)
    grad_active = dot(grad_out, down_w, ((1,), (1,)))
    grad_hidden_in = (grad_active * slope.astype(f32)).astype(bf16)
    up_grad = dot(second_in, grad_hidden_in, ((0,), (0,))).astype(bf16)
    up_grad = up_grad.reshape(n, r, q, width).transpose(0, 2, 1, 3).reshape(n, q * r, width)
    both_grads = jnp.concatenate([down_grad, up_grad], axis=1)
    grad_hidden_in = tie(grad_hidden_in, both_grads)
    both_grads = lax.psum_scatter(both_grads, "dp", scatter_dimension=0, tiled=True)
    both_grads = lax.psum_scatter(both_grads, "seq", scatter_dimension=0, tiled=True)
    both_grads = both_grads.reshape(-1, width).astype(f32)
    down_weight_grad = both_grads[: q * r]
    up_weight_grad = both_grads[q * r :].reshape(q, r, width).transpose(1, 0, 2).reshape(r, -1)
    up_bias_grad = jnp.sum(grad_hidden_in.astype(f32), axis=0)
    grad_second = dot(grad_hidden_in, up_w, ((1,), (1,)))
    grad_float = grad_out.astype(f32)
    down_bias_grad = jnp.sum(grad_float, axis=0)
    grad_middle_part, gain_two_grad, shift_two_grad = second_back(grad_second)
    grad_middle = grad_float + grad_middle_part
    grad_proj = grad_middle.astype(bf16)
    proj_bias_grad = jnp.sum(grad_proj.astype(f32), axis=0)
    grad_attended = dot(grad_proj, proj_w, ((1,), (1,))).astype(bf16)

    output = (middle + dot(active_in, down_w, ((1,), (0,))) + down_b).astype(bf16)
    grad_attended = tie(grad_attended, output)
    grads = attend_back(
        queries, own_kv, far_kv, attended, grad_attended, logsum, own_slots, slots
    )
    dq, own, far = grads
    far = grid.swap(far, 1)
    proj_grad = dot(tie(attended, dq), grad_proj, ((0,), (0,))).astype(bf16)
    both = (own + far.astype(f32)).astype(bf16)
    dqkv = jnp.concatenate([dq, both[0], both[1]], axis=1)
    split = 2 * width
    qk_s = Scatter(grid, dot(first_in, dqkv[:, :split], ((0,), (0,))).astype(bf16), order_a)
    v_grad = dot(first_in, dqkv[:, split:], ((0,), (0,))).astype(bf16)
    dqkv = tie(dqkv, qk_s.sent)
    query_bias_grad = jnp.sum(dqkv[:, :width].astype(f32), axis=0)
    value_bias_grad = jnp.sum(dqkv[:, split:].astype(f32), axis=0)
    grad_first = dot(dqkv, qkv_w, ((1,), (1,)))
    grad_input_part, gain_one_grad, shift_one_grad = norm_back(grad_first)
    input_grad = (grad_middle + grad_input_part).astype(bf16)

    small_grads = [
        gain_one_grad,
        shift_one_grad,
        query_bias_grad,
        value_bias_grad,
        proj_bias_grad,
        gain_two_grad,
        shift_two_grad,
        down_bias_grad,
    ]
    columns = jnp.concatenate(
        [jnp.stack(small_grads, axis=1), up_bias_grad.reshape(width, -1)], axis=1
    )
    taken = columns.shape[1]
    columns = jnp.pad(columns, ((0, 0), (0, LANES - taken)))
    v_s = Scatter(grid, jnp.concatenate([v_grad, proj_grad, columns.astype(bf16)], axis=1), order_b)
    input_grad = grid.from_packs(tie(input_grad, v_s.sent))
    block_out = grid.from_packs(output, v_s.sent)
    packed = jnp.concatenate([qk_s.last(), v_s.last()], axis=2)
    packed = Along(grid, packed).finish()
    qkv_weight_grad, proj_weight_grad = packed[:, : 3 * width], packed[:, 3 * width : 4 * width]
    columns = packed[:, 4 * width :]
    (
        gain_one_grad,
        shift_one_grad,
        query_bias_grad,
        value_bias_grad,
        proj_bias_grad,
        gain_two_grad,
        shift_two_grad,
        down_bias_grad,
    ) = [columns[:, j] for j in range(len(small))]
    up_bias_grad = columns[:, len(small) : taken].reshape(-1)
    return (
        block_out[None],
        input_grad[None],
        gain_one_grad,
        shift_one_grad,
        qkv_weight_grad,
        query_bias_grad,
        value_bias_grad,
        proj_weight_grad,
        proj_bias_grad,
        gain_two_grad,
        shift_two_grad,
        up_weight_grad,
        up_bias_grad,
        down_weight_grad,
        down_bias_grad,
    )


def solution(mesh):
    tokens = P("dp", None, "seq", None)
    vector = P(("dp", "seq"))
    matrix = P(("dp", "seq"), None)
    dp, seq = mesh.shape["dp"], mesh.shape["seq"]
    kinds = (
        vector,
        vector,
        matrix,
        vector,
        vector,
        matrix,
        vector,
        vector,
        vector,
        matrix,
        vector,
        matrix,
        vector,
    )
    return jax.shard_map(
        lambda *args: local(*args, dp=dp, seq=seq),
        mesh=mesh,
        in_specs=(tokens, tokens, P("dp", None, None)) + kinds,
        out_specs=(tokens, tokens) + kinds,
        check_vma=False,
    )
```

```python
import math

import jax
import jax.numpy as jnp
from jax import lax
from jax.experimental import pallas as pl
from jax.experimental.pallas import tpu as pltpu
from jax.sharding import PartitionSpec as P

HD = 64
LANES = 128
f32 = jnp.float32
bf16 = jnp.bfloat16

tail_cells = 3
closed = -1e30
norm_eps = 1e-06


def dot(left, right, contract):
    return lax.dot_general(left, right, (contract, ((), ())), preferred_element_type=f32)


def tie(value, *others):
    return lax.optimization_barrier((value,) + others)[0]


def layer_norm(values, gain, shift):
    center = values - jnp.mean(values, axis=-1, keepdims=True)
    spread = jnp.mean(center * center, axis=-1, keepdims=True)
    return center * lax.rsqrt(spread + norm_eps) * gain + shift


def slot_numbers(lens, places):
    widths = jnp.where(lens > 0, lens + tail_cells, 0)
    starts = jnp.cumsum(widths) - widths
    inside = (places[None, :] >= starts[:, None]) & (places[None, :] < (starts + lens)[:, None])
    labels = jnp.arange(lens.shape[0], dtype=jnp.int32) + 1
    return jnp.sum(jnp.where(inside, labels[:, None], 0), axis=0) - 1


class Grid:
    def __init__(self, dp, seq, micro):
        assert dp & (dp - 1) == 0 and seq == 2 * micro
        self.dp, self.seq, self.micro = dp, seq, micro
        self.bits = [1 << k for k in range(1, dp.bit_length() - 1)]
        self.d = lax.axis_index("dp")
        self.s = lax.axis_index("seq")

    def swap(self, value, bit):
        return lax.ppermute(value, "dp", [(k, k ^ bit) for k in range(self.dp)])

    def turn(self, value, step):
        return lax.ppermute(value, "seq", [(k, (k + step) % self.seq) for k in range(self.seq)])

    def routes(self):
        found = []
        half = self.seq // 2
        for p in range(self.micro):
            pairs = []
            for c in range(self.dp // 2):
                for a in range(2):
                    for s in range(self.seq):
                        m = (s + p) % self.micro
                        k, z = s // half, a * self.micro + m
                        pairs.append(((2 * c + a) * self.seq + s, (2 * c + k) * self.seq + z))
            found.append(pairs)
        return found

    def pick(self, blocks, index):
        return lax.dynamic_index_in_dim(blocks, index, 0, keepdims=False)

    def to_packs(self, blocks, *late):
        got = [
            lax.ppermute(self.pick(blocks, (self.s + p) % self.micro), ("dp", "seq"), pairs)
            for p, pairs in enumerate(self.routes())
        ]
        return jnp.concatenate([tie(part, *late) for part in got], axis=0)

    def from_packs(self, rows, *late):
        parts = rows.reshape(self.micro, -1, rows.shape[-1])
        got = [
            lax.ppermute(parts[p], ("dp", "seq"), [(b, a) for a, b in pairs])
            for p, pairs in enumerate(self.routes())
        ]
        got = jnp.stack([tie(part, *late) for part in got])
        return jnp.roll(got, self.s % self.micro, axis=0)

    def quarters(self, core):
        own = self.s % self.micro
        half = self.seq // 2
        return [half * core + (own - p) % self.micro for p in range(self.micro)]


class Gather:
    def __init__(self, grid, shard, streams, after=(), late=()):
        self.grid, self.rows = grid, grid.seq * shard.shape[0]
        shard = tie(shard, *after)
        blocks = [shard]
        blocks += [tie(grid.turn(shard, step), *late) for step in range(1, grid.seq)]
        self.streams = []
        start = 0
        for width, order in streams:
            parts = [block[:, start : start + width] for block in blocks]
            stacked = jnp.stack(parts[::-1] + parts[::-1])
            value = lax.dynamic_slice_in_dim(
                stacked, (grid.seq - 1 - grid.s) % grid.seq, grid.seq, 0
            )
            self.streams.append([value.reshape(1, self.rows, width), list(order) + [1], []])
            start += width

    def step(self, *late):
        for stream in self.streams:
            self.move(stream, *late)

    def move(self, stream, *late):
        g = self.grid
        value, order, done = stream
        bit = order.pop(0)
        other = tie(g.swap(value, bit), *late)
        low = (g.d & bit) == 0
        outer = 1 << sum(1 for have in done if have > bit)
        shape = (outer, 1, -1, self.rows, value.shape[-1])
        value, other = value.reshape(shape), other.reshape(shape)
        both = [jnp.where(low, value, other), jnp.where(low, other, value)]
        stream[0] = jnp.concatenate(both, axis=1).reshape(-1, self.rows, shape[-1])
        done.append(bit)

    def values(self):
        return [stream[0] for stream in self.streams]

    def finish(self, *late):
        while self.streams[0][1]:
            self.step(*late)
        return [value.reshape(-1, value.shape[-1]) for value in self.values()]


class Scatter:
    def __init__(self, grid, grad, order):
        self.grid, self.order = grid, [1] + list(order)
        self.left = sorted(self.order, reverse=True)
        self.value = grad
        self.rows = grad.shape[0] // (grid.dp * grid.seq)
        self.width = grad.shape[1]
        self.send()

    def send(self):
        g = self.grid
        bit = self.order.pop(0)
        at = self.left.index(bit)
        self.left.remove(bit)
        split = self.value.reshape(1 << at, 2, -1, self.width)
        mine = ((g.d & bit) != 0).astype(jnp.int32)
        self.sent = lax.dynamic_index_in_dim(split, 1 - mine, 1, keepdims=False).astype(bf16)
        self.kept = lax.dynamic_index_in_dim(split, mine, 1, keepdims=False)
        self.arriving = g.swap(self.sent, bit)

    def step(self):
        self.value = self.kept.astype(f32) + self.arriving.astype(f32)
        if self.order:
            self.send()
            return self.sent
        self.value = self.value.reshape(self.grid.seq, self.rows, self.width)
        return None

    def last(self):
        while self.step() is not None:
            pass
        return self.value


class Along:
    def __init__(self, grid, parts):
        self.own = grid.pick(parts, grid.s).astype(f32)
        steps = range(1, grid.seq)
        self.sent = [grid.pick(parts, (grid.s + step) % grid.seq).astype(bf16) for step in steps]
        self.got = [grid.turn(part, step) for part, step in zip(self.sent, steps)]

    def finish(self, *late):
        return self.own + sum(tie(part, *late).astype(f32) for part in self.got)


def attention_bias(row_ref, col_ref, bias):
    @pl.when(pl.program_id(0) == 0)
    def _():
        bias[...] = jnp.where(col_ref[...] == row_ref[...], 0.0, closed)


def head_lanes(value, head):
    lanes = lax.broadcasted_iota(jnp.int32, value.shape, 1)
    return jnp.where(lanes // HD == head, value, jnp.zeros_like(value))


def attend_kernel(row, col, q, k_own, v_own, k_far, v_far, out, logsum, bias):
    attention_bias(row, col, bias)
    n = q.shape[0]
    turned = []
    v_turned = [v_own[...].T, v_far[...].T]
    for h in range(LANES // HD):
        masked = head_lanes(q[...], h)
        scores = [
            dot(k[...], masked, ((1,), (1,))) + bias[pl.ds(j * n, n), :]
            for j, k in enumerate((k_own, k_far))
        ]
        highest = jnp.maximum(
            jnp.max(scores[0], axis=0, keepdims=True), jnp.max(scores[1], axis=0, keepdims=True)
        )
        expos = [jnp.exp(s - highest) for s in scores]
        totals = sum(jnp.sum(e, axis=0, keepdims=True) for e in expos)
        mixed = sum(
            dot(v[h * HD : (h + 1) * HD], e.astype(bf16), ((1,), (0,)))
            for v, e in zip(v_turned, expos)
        )
        turned.append(mixed / totals)
        logsum[h] = highest + jnp.log(totals)
    out[...] = jnp.concatenate(turned, axis=0).T.astype(bf16)


def attend_back_kernel(
    row, col, q, k_own, v_own, k_far, v_far, attended, grad, logsum,
    dq, own, far, bias,
):
    attention_bias(row, col, bias)
    n = q.shape[0]
    both = (grad[...].astype(f32) * attended[...].astype(f32)).T
    k_turned = [k_own[...].T, k_far[...].T]
    dq_turned = []
    dks, dvs = [0.0, 0.0], [0.0, 0.0]
    for h in range(LANES // HD):
        masked_q, masked_g = head_lanes(q[...], h), head_lanes(grad[...], h)
        inner = jnp.sum(both[h * HD : (h + 1) * HD], axis=0, keepdims=True)
        dq_head = 0.0
        for j, (k, v) in enumerate(((k_own, v_own), (k_far, v_far))):
            scores = dot(k[...], masked_q, ((1,), (1,))) + bias[pl.ds(j * n, n), :]
            chances = jnp.exp(scores - logsum[h])
            grad_chances = dot(v[...], masked_g, ((1,), (1,)))
            dvs[j] = dvs[j] + dot(chances.astype(bf16), masked_g, ((1,), (0,)))
            grad_scores = (chances * (grad_chances - inner)).astype(bf16)
            dks[j] = dks[j] + dot(grad_scores, masked_q, ((1,), (0,)))
            dq_head = dq_head + dot(
                k_turned[j][h * HD : (h + 1) * HD], grad_scores, ((1,), (0,))
            )
        dq_turned.append(dq_head)
    dq[...] = (jnp.concatenate(dq_turned, axis=0).T * (1.0 / math.sqrt(HD))).astype(dq.dtype)
    own[0], own[1] = dks[0], dvs[0]
    far[0], far[1] = dks[1].astype(far.dtype), dvs[1].astype(far.dtype)


def attention_specs(n, width):
    def at(offset):
        return pl.BlockSpec((n, LANES), lambda j: (0, offset + j))

    row = pl.BlockSpec((1, n), lambda j: (0, 0))
    col = pl.BlockSpec((2 * n, 1), lambda j: (0, 0))
    return [row, col, at(0), at(0), at(width // LANES), at(0), at(width // LANES)], at


def attend(queries, own_kv, far_kv, own_slots, slots):
    n, width = queries.shape
    specs, at = attention_specs(n, width)
    heads = LANES // HD
    return pl.pallas_call(
        attend_kernel,
        grid=(width // LANES,),
        in_specs=specs,
        out_specs=[at(0), pl.BlockSpec((heads, 1, n), lambda j: (j, 0, 0))],
        out_shape=[
            jax.ShapeDtypeStruct((n, width), bf16),
            jax.ShapeDtypeStruct((width // HD, 1, n), f32),
        ],
        scratch_shapes=[pltpu.VMEM((2 * n, n), f32)],
        name="attend",
    )(own_slots[None], slots[:, None], queries, own_kv, own_kv, far_kv, far_kv)


def attend_back(queries, own_kv, far_kv, attended, grad, logsum, own_slots, slots):
    n, width = queries.shape
    specs, at = attention_specs(n, width)
    heads = LANES // HD
    pair = pl.BlockSpec((2, n, LANES), lambda j: (0, 0, j))
    return pl.pallas_call(
        attend_back_kernel,
        grid=(width // LANES,),
        in_specs=specs
        + [at(0), at(0), pl.BlockSpec((heads, 1, n), lambda j: (j, 0, 0))],
        out_specs=[at(0), pair, pair],
        out_shape=[
            jax.ShapeDtypeStruct((n, width), bf16),
            jax.ShapeDtypeStruct((2, n, width), f32),
            jax.ShapeDtypeStruct((2, n, width), bf16),
        ],
        scratch_shapes=[pltpu.VMEM((2 * n, n), f32)],
        name="attend_back",
    )(
        own_slots[None],
        slots[:, None],
        queries,
        own_kv,
        own_kv,
        far_kv,
        far_kv,
        attended,
        grad,
        logsum,
    )


def local(
    tokens,
    cotangent,
    lengths,
    gain_one,
    shift_one,
    qkv_weight,
    query_bias,
    value_bias,
    proj_weight,
    proj_bias,
    gain_two,
    shift_two,
    up_weight,
    up_bias,
    down_weight,
    down_bias,
    *,
    dp,
    seq,
):
    micro, block, width = tokens.shape[1:]
    grid = Grid(dp, seq, micro)
    r = qkv_weight.shape[0]
    order_a, order_b = grid.bits, grid.bits[::-1]

    n, hidden_width = dp * seq, up_weight.shape[1]
    q = hidden_width // width

    up_rows = up_weight.reshape(r, q, width).transpose(1, 0, 2).reshape(q * r, width)
    others = lax.all_gather(
        jnp.concatenate([up_rows, down_weight], axis=0), ("dp", "seq"), axis=0, tiled=False
    )

    small = [gain_one, shift_one, query_bias, value_bias, proj_bias, gain_two, shift_two, down_bias]
    taken = len(small) + q
    columns = jnp.concatenate([jnp.stack(small), up_bias.reshape(q, r)], axis=0)
    columns = jnp.pad(columns, ((0, LANES - taken), (0, 0))).T
    packed = jnp.concatenate([qkv_weight, proj_weight, columns], axis=1)
    cut = 2 * width

    first_g = Gather(grid, packed, ((cut, order_a), (packed.shape[1] - cut, order_b)))
    inputs = grid.to_packs(tokens[0])
    first_half, second_half = first_g.finish()
    proj_w = second_half[:, width : 2 * width]
    rows = second_half[:, 2 * width :].T[:taken].astype(f32)
    gain_one_f, shift_one_f, query_b, value_b, proj_b, gain_two_f, shift_two_f, down_b = rows[
        : len(small)
    ]
    up_b = rows[len(small) :].reshape(q, n, r).transpose(1, 0, 2).reshape(-1)

    core = grid.d % 2
    away = grid.swap(lengths[0], 1)
    lens = jnp.where(grid.s // micro == core, lengths[0], away)
    lens = grid.pick(lens, grid.s % micro)
    spots = jnp.arange(block, dtype=jnp.int32)
    own_slots = slot_numbers(lens, jnp.concatenate([q * block + spots for q in grid.quarters(core)]))
    far_slots = slot_numbers(
        lens, jnp.concatenate([q * block + spots for q in grid.quarters(1 - core)])
    )
    slots = jnp.concatenate([own_slots, far_slots])

    inputs_f = inputs.astype(f32)
    normed, norm_back = jax.vjp(layer_norm, inputs_f, gain_one_f, shift_one_f)
    first_in = normed.astype(bf16)
    made = dot(first_in, first_half, ((1,), (0,)))
    queries = (made[:, :width] + query_b).astype(bf16) * bf16(1.0 / math.sqrt(HD))
    value_w = second_half[:, :width]
    made_values = dot(first_in, value_w, ((1,), (0,))) + value_b
    own_kv = jnp.concatenate([made[:, width:], made_values], axis=1).astype(bf16)
    far_kv = grid.swap(own_kv, 1)
    attended, logsum = attend(queries, own_kv, far_kv, own_slots, slots)
    grad_out = grid.to_packs(tie(cotangent[0], own_kv), attended)
    others = tie(others, attended)
    up_w = jnp.concatenate(
        [others[:, j * r : (j + 1) * r].reshape(width, width) for j in range(q)], axis=1
    )
    down_w = others[:, q * r :].reshape(hidden_width, width)

    middle = inputs_f + dot(attended, proj_w, ((1,), (0,))) + proj_b
    second, second_back = jax.vjp(layer_norm, middle, gain_two_f, shift_two_f)
    second_in = second.astype(bf16)
    hidden = dot(second_in, up_w, ((1,), (0,))) + up_b
    share = 0.5 * (1.0 + lax.erf(hidden * math.sqrt(0.5)))
    bell = jnp.exp(-0.5 * hidden * hidden) * (1.0 / math.sqrt(2.0 * math.pi))
    active_in, slope = lax.optimization_barrier(
        ((hidden * share).astype(bf16), (share + hidden * bell).astype(bf16))
    )

    down_grad = dot(active_in, grad_out, ((0,), (0,))).astype(bf16).reshape(n, q * r, width)
    grad_active = dot(grad_out, down_w, ((1,), (1,)))
    grad_hidden_in = (grad_active * slope.astype(f32)).astype(bf16)
    up_grads = [
        dot(second_in, grad_hidden_in[:, j * width : (j + 1) * width], ((0,), (0,)))
        .astype(bf16)
        .reshape(n, r, width)
        for j in range(q)
    ]
    both_grads = jnp.concatenate([down_grad] + up_grads, axis=1)
    grad_hidden_in = tie(grad_hidden_in, both_grads)
    both_grads = lax.psum_scatter(both_grads, "dp", scatter_dimension=0, tiled=True)
    over_dp = both_grads
    both_grads = lax.psum_scatter(both_grads, "seq", scatter_dimension=0, tiled=True)
    both_grads = both_grads.reshape(-1, width).astype(f32)
    down_weight_grad = both_grads[: q * r]
    up_weight_grad = both_grads[q * r :].reshape(q, r, width).transpose(1, 0, 2).reshape(r, -1)
    up_bias_grad = jnp.sum(grad_hidden_in.astype(f32), axis=0)
    grad_second = dot(grad_hidden_in, up_w, ((1,), (1,)))
    grad_float = grad_out.astype(f32)
    down_bias_grad = jnp.sum(grad_float, axis=0)
    grad_middle_part, gain_two_grad, shift_two_grad = second_back(grad_second)
    grad_middle = grad_float + grad_middle_part
    grad_proj = grad_middle.astype(bf16)
    proj_bias_grad = jnp.sum(grad_proj.astype(f32), axis=0)
    grad_attended = dot(grad_proj, proj_w, ((1,), (1,))).astype(bf16)

    output = (middle + dot(active_in, down_w, ((1,), (0,))) + down_b).astype(bf16)
    grad_attended = tie(grad_attended, output)
    grads = attend_back(
        queries, own_kv, far_kv, attended, grad_attended, logsum, own_slots, slots
    )
    dq, own, far = grads
    block_out = grid.from_packs(output, dq)
    far = grid.swap(tie(far, block_out), 1)
    proj_grad = dot(tie(attended, dq), grad_proj, ((0,), (0,))).astype(bf16)
    both = (own + far.astype(f32)).astype(bf16)
    dqkv = jnp.concatenate([dq, both[0], both[1]], axis=1)
    split = 2 * width
    qk_s = Scatter(grid, dot(first_in, dqkv[:, :split], ((0,), (0,))).astype(bf16), order_a)
    v_grad = dot(first_in, dqkv[:, split:], ((0,), (0,))).astype(bf16)
    dqkv = tie(dqkv, qk_s.sent)
    query_bias_grad = jnp.sum(dqkv[:, :width].astype(f32), axis=0)
    value_bias_grad = jnp.sum(dqkv[:, split:].astype(f32), axis=0)
    grad_first = dot(dqkv[:, :split], first_half, ((1,), (1,)))
    grad_first = grad_first + dot(dqkv[:, split:], value_w, ((1,), (1,)))
    grad_input_part, gain_one_grad, shift_one_grad = norm_back(grad_first)
    input_grad = (grad_middle + grad_input_part).astype(bf16)

    small_grads = [
        gain_one_grad,
        shift_one_grad,
        query_bias_grad,
        value_bias_grad,
        proj_bias_grad,
        gain_two_grad,
        shift_two_grad,
        down_bias_grad,
    ]
    columns = jnp.concatenate(
        [
            jnp.stack(small_grads),
            up_bias_grad.reshape(n, q, r).transpose(1, 0, 2).reshape(q, width),
        ],
        axis=0,
    ).astype(bf16)
    columns = jnp.pad(columns, ((0, LANES - taken), (0, 0))).T
    columns, v_grad, proj_grad = lax.optimization_barrier((columns, v_grad, proj_grad))
    v_s = Scatter(grid, tie(jnp.concatenate([v_grad, proj_grad, columns], axis=1), over_dp), order_b)
    input_grad = grid.from_packs(tie(input_grad, v_s.sent))
    packed = jnp.concatenate([qk_s.last(), v_s.last()], axis=2)
    packed = Along(grid, tie(packed, both_grads)).finish()
    qkv_weight_grad, proj_weight_grad = packed[:, : 3 * width], packed[:, 3 * width : 4 * width]
    rows = packed[:, 4 * width :].T[:taken]
    (
        gain_one_grad,
        shift_one_grad,
        query_bias_grad,
        value_bias_grad,
        proj_bias_grad,
        gain_two_grad,
        shift_two_grad,
        down_bias_grad,
    ) = rows[: len(small)]
    up_bias_grad = rows[len(small) :].reshape(-1)
    return (
        block_out[None],
        input_grad[None],
        gain_one_grad,
        shift_one_grad,
        qkv_weight_grad,
        query_bias_grad,
        value_bias_grad,
        proj_weight_grad,
        proj_bias_grad,
        gain_two_grad,
        shift_two_grad,
        up_weight_grad,
        up_bias_grad,
        down_weight_grad,
        down_bias_grad,
    )


def solution(mesh):
    tokens = P("dp", None, "seq", None)
    vector = P(("dp", "seq"))
    matrix = P(("dp", "seq"), None)
    dp, seq = mesh.shape["dp"], mesh.shape["seq"]
    kinds = (
        vector,
        vector,
        matrix,
        vector,
        vector,
        matrix,
        vector,
        vector,
        vector,
        matrix,
        vector,
        matrix,
        vector,
    )
    return jax.shard_map(
        lambda *args: local(*args, dp=dp, seq=seq),
        mesh=mesh,
        in_specs=(tokens, tokens, P("dp", None, None)) + kinds,
        out_specs=(tokens, tokens) + kinds,
        check_vma=False,
    )
```

```python
import math

import jax
import jax.numpy as jnp
from jax import lax
from jax.experimental import pallas as pl
from jax.experimental.pallas import tpu as pltpu
from jax.sharding import PartitionSpec as P

HD = 64
LANES = 128
f32 = jnp.float32
bf16 = jnp.bfloat16

tail_cells = 3
closed = -1e30
norm_eps = 1e-06


def dot(left, right, contract):
    return lax.dot_general(left, right, (contract, ((), ())), preferred_element_type=f32)


def tie(value, *others):
    return lax.optimization_barrier((value,) + others)[0]


def layer_norm(values, gain, shift):
    center = values - jnp.mean(values, axis=-1, keepdims=True)
    spread = jnp.mean(center * center, axis=-1, keepdims=True)
    return center * lax.rsqrt(spread + norm_eps) * gain + shift


def slot_numbers(lens, places):
    widths = jnp.where(lens > 0, lens + tail_cells, 0)
    starts = jnp.cumsum(widths) - widths
    inside = (places[None, :] >= starts[:, None]) & (places[None, :] < (starts + lens)[:, None])
    labels = jnp.arange(lens.shape[0], dtype=jnp.int32) + 1
    return jnp.sum(jnp.where(inside, labels[:, None], 0), axis=0) - 1


class Grid:
    def __init__(self, dp, seq, micro):
        assert dp & (dp - 1) == 0 and seq == 2 * micro
        self.dp, self.seq, self.micro = dp, seq, micro
        self.bits = [1 << k for k in range(1, dp.bit_length() - 1)]
        self.d = lax.axis_index("dp")
        self.s = lax.axis_index("seq")

    def swap(self, value, bit):
        return lax.ppermute(value, "dp", [(k, k ^ bit) for k in range(self.dp)])

    def turn(self, value, step):
        return lax.ppermute(value, "seq", [(k, (k + step) % self.seq) for k in range(self.seq)])

    def routes(self):
        found = []
        half = self.seq // 2
        for p in range(self.micro):
            pairs = []
            for c in range(self.dp // 2):
                for a in range(2):
                    for s in range(self.seq):
                        m = (s + p) % self.micro
                        k, z = s // half, a * self.micro + m
                        pairs.append(((2 * c + a) * self.seq + s, (2 * c + k) * self.seq + z))
            found.append(pairs)
        return found

    def pick(self, blocks, index):
        return lax.dynamic_index_in_dim(blocks, index, 0, keepdims=False)

    def to_packs(self, blocks, *late):
        got = [
            lax.ppermute(self.pick(blocks, (self.s + p) % self.micro), ("dp", "seq"), pairs)
            for p, pairs in enumerate(self.routes())
        ]
        return jnp.concatenate([tie(part, *late) for part in got], axis=0)

    def from_packs(self, rows, *late):
        parts = rows.reshape(self.micro, -1, rows.shape[-1])
        got = [
            lax.ppermute(parts[p], ("dp", "seq"), [(b, a) for a, b in pairs])
            for p, pairs in enumerate(self.routes())
        ]
        got = jnp.stack([tie(part, *late) for part in got])
        return jnp.roll(got, self.s % self.micro, axis=0)

    def quarters(self, core):
        own = self.s % self.micro
        half = self.seq // 2
        return [half * core + (own - p) % self.micro for p in range(self.micro)]


class Gather:
    def __init__(self, grid, shard, streams, after=(), late=()):
        self.grid, self.rows = grid, grid.seq * shard.shape[0]
        shard = tie(shard, *after)
        blocks = [shard]
        blocks += [tie(grid.turn(shard, step), *late) for step in range(1, grid.seq)]
        self.streams = []
        start = 0
        for width, order in streams:
            parts = [block[:, start : start + width] for block in blocks]
            stacked = jnp.stack(parts[::-1] + parts[::-1])
            value = lax.dynamic_slice_in_dim(
                stacked, (grid.seq - 1 - grid.s) % grid.seq, grid.seq, 0
            )
            self.streams.append([value.reshape(1, self.rows, width), list(order) + [1], []])
            start += width

    def step(self, *late):
        for stream in self.streams:
            self.move(stream, *late)

    def move(self, stream, *late):
        g = self.grid
        value, order, done = stream
        bit = order.pop(0)
        other = tie(g.swap(value, bit), *late)
        low = (g.d & bit) == 0
        outer = 1 << sum(1 for have in done if have > bit)
        shape = (outer, 1, -1, self.rows, value.shape[-1])
        value, other = value.reshape(shape), other.reshape(shape)
        both = [jnp.where(low, value, other), jnp.where(low, other, value)]
        stream[0] = jnp.concatenate(both, axis=1).reshape(-1, self.rows, shape[-1])
        done.append(bit)

    def values(self):
        return [stream[0] for stream in self.streams]

    def finish(self, *late):
        while self.streams[0][1]:
            self.step(*late)
        return [value.reshape(-1, value.shape[-1]) for value in self.values()]


class Scatter:
    def __init__(self, grid, grad, order):
        self.grid, self.order = grid, [1] + list(order)
        self.left = sorted(self.order, reverse=True)
        self.value = grad
        self.rows = grad.shape[0] // (grid.dp * grid.seq)
        self.width = grad.shape[1]
        self.send()

    def send(self):
        g = self.grid
        bit = self.order.pop(0)
        at = self.left.index(bit)
        self.left.remove(bit)
        split = self.value.reshape(1 << at, 2, -1, self.width)
        mine = ((g.d & bit) != 0).astype(jnp.int32)
        self.sent = lax.dynamic_index_in_dim(split, 1 - mine, 1, keepdims=False).astype(bf16)
        self.kept = lax.dynamic_index_in_dim(split, mine, 1, keepdims=False)
        self.arriving = g.swap(self.sent, bit)

    def step(self):
        self.value = self.kept.astype(f32) + self.arriving.astype(f32)
        if self.order:
            self.send()
            return self.sent
        self.value = self.value.reshape(self.grid.seq, self.rows, self.width)
        return None

    def last(self):
        while self.step() is not None:
            pass
        return self.value


class Along:
    def __init__(self, grid, parts):
        self.own = grid.pick(parts, grid.s).astype(f32)
        steps = range(1, grid.seq)
        self.sent = [grid.pick(parts, (grid.s + step) % grid.seq).astype(bf16) for step in steps]
        self.got = [grid.turn(part, step) for part, step in zip(self.sent, steps)]

    def finish(self, *late):
        return self.own + sum(tie(part, *late).astype(f32) for part in self.got)


def attention_bias(row_ref, col_ref, bias):
    @pl.when(pl.program_id(0) == 0)
    def _():
        bias[...] = jnp.where(col_ref[...] == row_ref[...], 0.0, closed)


def head_lanes(value, head):
    lanes = lax.broadcasted_iota(jnp.int32, value.shape, 1)
    return jnp.where(lanes // HD == head, value, jnp.zeros_like(value))


def attend_kernel(row, col, q, k_own, v_own, k_far, v_far, out, logsum, bias):
    attention_bias(row, col, bias)
    n = q.shape[0]
    turned = []
    v_turned = [v_own[...].T, v_far[...].T]
    for h in range(LANES // HD):
        masked = head_lanes(q[...], h)
        scores = [
            dot(k[...], masked, ((1,), (1,))) + bias[pl.ds(j * n, n), :]
            for j, k in enumerate((k_own, k_far))
        ]
        highest = jnp.maximum(
            jnp.max(scores[0], axis=0, keepdims=True), jnp.max(scores[1], axis=0, keepdims=True)
        )
        expos = [jnp.exp(s - highest) for s in scores]
        totals = sum(jnp.sum(e, axis=0, keepdims=True) for e in expos)
        mixed = sum(
            dot(v[h * HD : (h + 1) * HD], e.astype(bf16), ((1,), (0,)))
            for v, e in zip(v_turned, expos)
        )
        turned.append(mixed / totals)
        logsum[h] = highest + jnp.log(totals)
    out[...] = jnp.concatenate(turned, axis=0).T.astype(bf16)


def attend_back_kernel(
    row, col, q, k_own, v_own, k_far, v_far, attended, grad, logsum,
    dq, own, far, bias,
):
    attention_bias(row, col, bias)
    n = q.shape[0]
    both = (grad[...].astype(f32) * attended[...].astype(f32)).T
    k_turned = [k_own[...].T, k_far[...].T]
    dq_turned = []
    dks, dvs = [0.0, 0.0], [0.0, 0.0]
    for h in range(LANES // HD):
        masked_q, masked_g = head_lanes(q[...], h), head_lanes(grad[...], h)
        inner = jnp.sum(both[h * HD : (h + 1) * HD], axis=0, keepdims=True)
        dq_head = 0.0
        for j, (k, v) in enumerate(((k_own, v_own), (k_far, v_far))):
            scores = dot(k[...], masked_q, ((1,), (1,))) + bias[pl.ds(j * n, n), :]
            chances = jnp.exp(scores - logsum[h])
            grad_chances = dot(v[...], masked_g, ((1,), (1,)))
            dvs[j] = dvs[j] + dot(chances.astype(bf16), masked_g, ((1,), (0,)))
            grad_scores = (chances * (grad_chances - inner)).astype(bf16)
            dks[j] = dks[j] + dot(grad_scores, masked_q, ((1,), (0,)))
            dq_head = dq_head + dot(
                k_turned[j][h * HD : (h + 1) * HD], grad_scores, ((1,), (0,))
            )
        dq_turned.append(dq_head)
    dq[...] = (jnp.concatenate(dq_turned, axis=0).T * (1.0 / math.sqrt(HD))).astype(dq.dtype)
    own[0], own[1] = dks[0], dvs[0]
    far[0], far[1] = dks[1].astype(far.dtype), dvs[1].astype(far.dtype)


def attention_specs(n, width):
    def at(offset):
        return pl.BlockSpec((n, LANES), lambda j: (0, offset + j))

    row = pl.BlockSpec((1, n), lambda j: (0, 0))
    col = pl.BlockSpec((2 * n, 1), lambda j: (0, 0))
    return [row, col, at(0), at(0), at(width // LANES), at(0), at(width // LANES)], at


def attend(queries, own_kv, far_kv, own_slots, slots):
    n, width = queries.shape
    specs, at = attention_specs(n, width)
    heads = LANES // HD
    return pl.pallas_call(
        attend_kernel,
        grid=(width // LANES,),
        in_specs=specs,
        out_specs=[at(0), pl.BlockSpec((heads, 1, n), lambda j: (j, 0, 0))],
        out_shape=[
            jax.ShapeDtypeStruct((n, width), bf16),
            jax.ShapeDtypeStruct((width // HD, 1, n), f32),
        ],
        scratch_shapes=[pltpu.VMEM((2 * n, n), f32)],
        name="attend",
    )(own_slots[None], slots[:, None], queries, own_kv, own_kv, far_kv, far_kv)


def attend_back(queries, own_kv, far_kv, attended, grad, logsum, own_slots, slots):
    n, width = queries.shape
    specs, at = attention_specs(n, width)
    heads = LANES // HD
    pair = pl.BlockSpec((2, n, LANES), lambda j: (0, 0, j))
    return pl.pallas_call(
        attend_back_kernel,
        grid=(width // LANES,),
        in_specs=specs
        + [at(0), at(0), pl.BlockSpec((heads, 1, n), lambda j: (j, 0, 0))],
        out_specs=[at(0), pair, pair],
        out_shape=[
            jax.ShapeDtypeStruct((n, width), bf16),
            jax.ShapeDtypeStruct((2, n, width), f32),
            jax.ShapeDtypeStruct((2, n, width), bf16),
        ],
        scratch_shapes=[pltpu.VMEM((2 * n, n), f32)],
        name="attend_back",
    )(
        own_slots[None],
        slots[:, None],
        queries,
        own_kv,
        own_kv,
        far_kv,
        far_kv,
        attended,
        grad,
        logsum,
    )


def local(
    tokens,
    cotangent,
    lengths,
    gain_one,
    shift_one,
    qkv_weight,
    query_bias,
    value_bias,
    proj_weight,
    proj_bias,
    gain_two,
    shift_two,
    up_weight,
    up_bias,
    down_weight,
    down_bias,
    *,
    dp,
    seq,
):
    micro, block, width = tokens.shape[1:]
    grid = Grid(dp, seq, micro)
    r = qkv_weight.shape[0]
    order_a, order_b = grid.bits, grid.bits[::-1]

    n, hidden_width = dp * seq, up_weight.shape[1]
    q = hidden_width // width

    up_rows = up_weight.reshape(r, q, width).transpose(1, 0, 2).reshape(q * r, width)
    others = lax.all_gather(
        jnp.concatenate([up_rows, down_weight], axis=0), ("dp", "seq"), axis=0, tiled=False
    )

    small = [gain_one, shift_one, query_bias, value_bias, proj_bias, gain_two, shift_two, down_bias]
    taken = len(small) + q
    columns = jnp.concatenate([jnp.stack(small), up_bias.reshape(q, r)], axis=0)
    columns = jnp.pad(columns, ((0, LANES - taken), (0, 0))).T
    packed = jnp.concatenate([qkv_weight, proj_weight, columns], axis=1)
    cut = 2 * width

    first_g = Gather(grid, packed, ((cut, order_a), (packed.shape[1] - cut, order_b)))
    inputs = grid.to_packs(tie(tokens[0], *first_g.values()))
    first_half, second_half = first_g.finish()
    proj_w = second_half[:, width : 2 * width]
    rows = second_half[:, 2 * width :].T[:taken].astype(f32)
    gain_one_f, shift_one_f, query_b, value_b, proj_b, gain_two_f, shift_two_f, down_b = rows[
        : len(small)
    ]
    up_b = rows[len(small) :].reshape(q, n, r).transpose(1, 0, 2).reshape(-1)

    core = grid.d % 2
    away = grid.swap(lengths[0], 1)
    lens = jnp.where(grid.s // micro == core, lengths[0], away)
    lens = grid.pick(lens, grid.s % micro)
    spots = jnp.arange(block, dtype=jnp.int32)
    own_slots = slot_numbers(lens, jnp.concatenate([q * block + spots for q in grid.quarters(core)]))
    far_slots = slot_numbers(
        lens, jnp.concatenate([q * block + spots for q in grid.quarters(1 - core)])
    )
    slots = jnp.concatenate([own_slots, far_slots])

    inputs_f = inputs.astype(f32)
    normed, norm_back = jax.vjp(layer_norm, inputs_f, gain_one_f, shift_one_f)
    first_in = normed.astype(bf16)
    made = dot(first_in, first_half, ((1,), (0,)))
    queries = (made[:, :width] + query_b).astype(bf16) * bf16(1.0 / math.sqrt(HD))
    value_w = second_half[:, :width]
    made_values = dot(first_in, value_w, ((1,), (0,))) + value_b
    own_kv = jnp.concatenate([made[:, width:], made_values], axis=1).astype(bf16)
    far_kv = grid.swap(own_kv, 1)
    attended, logsum = attend(queries, own_kv, far_kv, own_slots, slots)
    pulled = tie(cotangent[0], attended)
    others = tie(others, attended)
    up_w = jnp.concatenate(
        [others[:, j * r : (j + 1) * r].reshape(width, width) for j in range(q)], axis=1
    )
    down_w = others[:, q * r :].reshape(hidden_width, width)

    middle = inputs_f + dot(attended, proj_w, ((1,), (0,))) + proj_b
    second, second_back = jax.vjp(layer_norm, middle, gain_two_f, shift_two_f)
    second_in = second.astype(bf16)
    hidden = dot(second_in, up_w, ((1,), (0,))) + up_b
    share = 0.5 * (1.0 + lax.erf(hidden * math.sqrt(0.5)))
    bell = jnp.exp(-0.5 * hidden * hidden) * (1.0 / math.sqrt(2.0 * math.pi))
    active_in, slope = lax.optimization_barrier(
        ((hidden * share).astype(bf16), (share + hidden * bell).astype(bf16))
    )

    grad_out = grid.to_packs(pulled, active_in)
    down_grad = dot(active_in, grad_out, ((0,), (0,))).astype(bf16).reshape(n, q * r, width)
    grad_active = dot(grad_out, down_w, ((1,), (1,)))
    grad_hidden_in = (grad_active * slope.astype(f32)).astype(bf16)
    up_grads = [
        dot(second_in, grad_hidden_in[:, j * width : (j + 1) * width], ((0,), (0,)))
        .astype(bf16)
        .reshape(n, r, width)
        for j in range(q)
    ]
    both_grads = jnp.concatenate([down_grad] + up_grads, axis=1)
    grad_hidden_in = tie(grad_hidden_in, both_grads)
    both_grads = lax.psum_scatter(both_grads, "dp", scatter_dimension=0, tiled=True)
    over_dp = both_grads
    both_grads = lax.psum_scatter(both_grads, "seq", scatter_dimension=0, tiled=True)
    both_grads = both_grads.reshape(-1, width).astype(f32)
    down_weight_grad = both_grads[: q * r]
    up_weight_grad = both_grads[q * r :].reshape(q, r, width).transpose(1, 0, 2).reshape(r, -1)
    up_bias_grad = jnp.sum(grad_hidden_in.astype(f32), axis=0)
    grad_second = dot(grad_hidden_in, up_w, ((1,), (1,)))
    grad_float = grad_out.astype(f32)
    down_bias_grad = jnp.sum(grad_float, axis=0)
    grad_middle_part, gain_two_grad, shift_two_grad = second_back(grad_second)
    grad_middle = grad_float + grad_middle_part
    grad_proj = grad_middle.astype(bf16)
    proj_bias_grad = jnp.sum(grad_proj.astype(f32), axis=0)
    grad_attended = dot(grad_proj, proj_w, ((1,), (1,))).astype(bf16)

    output = (middle + dot(active_in, down_w, ((1,), (0,))) + down_b).astype(bf16)
    grad_attended = tie(grad_attended, output)
    grads = attend_back(
        queries, own_kv, far_kv, attended, grad_attended, logsum, own_slots, slots
    )
    dq, own, far = grads
    block_out = grid.from_packs(output, dq)
    far = grid.swap(tie(far, block_out), 1)
    proj_grad = dot(tie(attended, dq), grad_proj, ((0,), (0,))).astype(bf16)
    both = (own + far.astype(f32)).astype(bf16)
    dqkv = jnp.concatenate([dq, both[0], both[1]], axis=1)
    split = 2 * width
    qk_s = Scatter(grid, dot(first_in, dqkv[:, :split], ((0,), (0,))).astype(bf16), order_a)
    v_grad = dot(first_in, dqkv[:, split:], ((0,), (0,))).astype(bf16)
    dqkv = tie(dqkv, qk_s.sent)
    query_bias_grad = jnp.sum(dqkv[:, :width].astype(f32), axis=0)
    value_bias_grad = jnp.sum(dqkv[:, split:].astype(f32), axis=0)
    grad_first = dot(dqkv[:, :split], first_half, ((1,), (1,)))
    grad_first = grad_first + dot(dqkv[:, split:], value_w, ((1,), (1,)))
    grad_input_part, gain_one_grad, shift_one_grad = norm_back(grad_first)
    input_grad = (grad_middle + grad_input_part).astype(bf16)

    small_grads = [
        gain_one_grad,
        shift_one_grad,
        query_bias_grad,
        value_bias_grad,
        proj_bias_grad,
        gain_two_grad,
        shift_two_grad,
        down_bias_grad,
    ]
    columns = jnp.concatenate(
        [
            jnp.stack(small_grads),
            up_bias_grad.reshape(n, q, r).transpose(1, 0, 2).reshape(q, width),
        ],
        axis=0,
    ).astype(bf16)
    columns = jnp.pad(columns, ((0, LANES - taken), (0, 0))).T
    columns, v_grad, proj_grad = lax.optimization_barrier((columns, v_grad, proj_grad))
    v_s = Scatter(grid, tie(jnp.concatenate([v_grad, proj_grad, columns], axis=1), over_dp), order_b)
    input_grad = grid.from_packs(tie(input_grad, v_s.sent))
    packed = jnp.concatenate([qk_s.last(), v_s.last()], axis=2)
    packed = Along(grid, tie(packed, both_grads)).finish()
    qkv_weight_grad, proj_weight_grad = packed[:, : 3 * width], packed[:, 3 * width : 4 * width]
    rows = packed[:, 4 * width :].T[:taken]
    (
        gain_one_grad,
        shift_one_grad,
        query_bias_grad,
        value_bias_grad,
        proj_bias_grad,
        gain_two_grad,
        shift_two_grad,
        down_bias_grad,
    ) = rows[: len(small)]
    up_bias_grad = rows[len(small) :].reshape(-1)
    return (
        block_out[None],
        input_grad[None],
        gain_one_grad,
        shift_one_grad,
        qkv_weight_grad,
        query_bias_grad,
        value_bias_grad,
        proj_weight_grad,
        proj_bias_grad,
        gain_two_grad,
        shift_two_grad,
        up_weight_grad,
        up_bias_grad,
        down_weight_grad,
        down_bias_grad,
    )


def solution(mesh):
    tokens = P("dp", None, "seq", None)
    vector = P(("dp", "seq"))
    matrix = P(("dp", "seq"), None)
    dp, seq = mesh.shape["dp"], mesh.shape["seq"]
    kinds = (
        vector,
        vector,
        matrix,
        vector,
        vector,
        matrix,
        vector,
        vector,
        vector,
        matrix,
        vector,
        matrix,
        vector,
    )
    return jax.shard_map(
        lambda *args: local(*args, dp=dp, seq=seq),
        mesh=mesh,
        in_specs=(tokens, tokens, P("dp", None, None)) + kinds,
        out_specs=(tokens, tokens) + kinds,
        check_vma=False,
    )
```
